512 devices in a mesh: ctx: 64 (over z_hi, y, core), head: 8 (over z_lo, x).
Axes of the slice: x: 4, y: 8, z: 8 (z_hi: 4, z_lo: 2; z = z_hi * 2 + z_lo), core: 2. Of those that a mesh axis runs over, the one named last changes fastest.
Arguments:
- queries: bfloat16 [3072, 8192], P('ctx', 'head'), may hold values from -120 to 120
- cached_keys: bfloat16 [20480, 1024], P('ctx', 'head'), may hold values from -5 to 15
- cached_values: bfloat16 [20480, 1024], P('ctx', 'head'), may hold values from -6 to 6
- fresh_keys: bfloat16 [3072, 1024], P('ctx', 'head'), may hold values from -5 to 15
- fresh_values: bfloat16 [3072, 1024], P('ctx', 'head'), may hold values from -6 to 6
- recompute_index: int32 [64, 48], P('ctx'), may hold values from 0 to 319, as said below
- recompute_count: int32 [64], P('ctx'), may hold values from 1 to 48, 2688 in all
- group_offsets: int32 [64], replicated, may hold values from 0 to 40257, as said below
Outputs:
- attention: bfloat16 [3072, 8192], P('ctx', 'head')
- joined_keys: bfloat16 [20480, 1024], P('ctx', 'head')
- joined_values: bfloat16 [20480, 1024], P('ctx', 'head')
- drift: float32 [64, 48], P('ctx')
The draws below stay inside these ranges and needn't reach their ends.
Inputs may be any that keep to these rules, and one draw needn't show every extreme that they name: `recompute_index`: the entries of one group's row are different token numbers of that group. group_offsets[c + 1] - group_offsets[c] lies between 320 and 639.
All inputs are finite; a program needn't handle non-finite values. No bound on the sum of `recompute_count` on one device may be relied on, other than what follows from the above.
Results may differ from the reference program's by a relative error of at most 0.008.
Values may be sent and summed in bfloat16 or wider, within the bound.
No kernel may reach another device: no remote copies, remote signals or barrier semaphores. Data moves between devices by JAX's collectives and lax.ppermute only.
A program may use at most 64 MiB of HBM per device.

```python
import math
import jax
import jax.numpy as jnp
import numpy as np
from jax import lax

HEADS = 64
KV_HEADS = 8
HEAD_DIM = 128
GROUP_LEN = 320
R_MAX = 48
GROUPS = 64
TOKENS = 20480
ROWS = 3072


def key_draw(key, row_count, salt_value):
    width = KV_HEADS * HEAD_DIM
    noise = jnp.clip(jax.random.normal(jax.random.fold_in(key, salt_value), (row_count, width), jnp.float32), -5.0, 5.0)
    return noise


def draw_cached_keys(key, part):
    return key_draw(key, TOKENS, 11).astype(jnp.bfloat16)


def draw_fresh_keys(key, part):
    return key_draw(key, ROWS, 12).astype(jnp.bfloat16)


def draw_queries(key, part):
    width = HEADS * HEAD_DIM
    noise = jnp.clip(jax.random.normal(jax.random.fold_in(key, 13), (ROWS, width), jnp.float32) * 1.5, -9.0, 9.0)
    return noise.astype(jnp.bfloat16)


def draw_recompute_index(key, part):
    row_keys = jax.random.split(jax.random.fold_in(key, 21), GROUPS)

    def one_row(row_key):
        return jax.random.permutation(row_key, GROUP_LEN)[:R_MAX]
    return jax.vmap(one_row)(row_keys).astype(jnp.int32)


def draw_group_offsets(key, part):
    steps_between = GROUP_LEN + jax.random.randint(jax.random.fold_in(key, 31), (GROUPS,), 0, GROUP_LEN)
    steps_between = jnp.where(jnp.arange(GROUPS) == 0, 0, steps_between).astype(jnp.int32)
    running = jnp.cumsum(steps_between).astype(jnp.int32)
    final_start = (GROUPS - 1) * (2 * GROUP_LEN - 1)
    return (running + (final_start - running[GROUPS - 1])).astype(jnp.int32)


def levels(key, dims, pieces, least, top_value):
    loudness, own = 1.0, jax.random.fold_in(key, 6)
    for position, shards_of in pieces:
        heights = jnp.exp(jax.random.uniform(jax.random.fold_in(own, position), (shards_of,), jnp.float32, least / len(pieces), top_value / len(pieces)))
        loudness = loudness * jnp.repeat(heights, dims[position] // shards_of).reshape([-1 if axis == position else 1 for axis in range(len(dims))])
    return loudness


def profile(count, total, limit, skew):
    loads = [(1 << 20) // math.isqrt(rank ** skew) + 1 for rank in range(2, count + 1)]
    spare, given = total - limit - (count - 1), [1] * (count - 1)
    while spare > 0:
        candidates = [i for i in range(count - 1) if given[i] < limit]
        whole, left = sum([loads[i] for i in candidates]), spare
        for i in candidates:
            more = min(limit - given[i], max(1, left * loads[i] // whole), spare)
            given[i] = given[i] + more
            spare = spare - more
    return np.array([limit] + given)


def uneven(key, count, total, reach, skew):
    if count == 2:
        one = jax.random.randint(key, (), max(1, total - reach), min(reach, total - 1) + 1)
        return jnp.stack([one, total - one])
    sizes = jnp.asarray(profile(count, total, reach, skew), jnp.int32)
    couples = (count - 1) // 2
    source_of, taker = sizes[1:1 + 2 * couples:2], sizes[2:2 + 2 * couples:2]
    slack = jnp.minimum(source_of - 1, reach - taker)
    moved = jax.random.randint(jax.random.fold_in(key, 1), (couples,), 0, 1 << 20) % (slack + 1)
    sizes = sizes.at[1:1 + 2 * couples:2].set(source_of - moved).at[2:2 + 2 * couples:2].set(taker + moved)
    return sizes[jax.random.permutation(jax.random.fold_in(key, 2), count)]


def normal_values(own_key, extent, scale, most, pieces=(), kind=jnp.bfloat16):
    level = levels(own_key, extent, pieces, -0.22, 0.18) if pieces else 1.0
    drawn = jax.random.normal(own_key, extent, jnp.float32) * scale * level
    return jnp.minimum(jnp.maximum(drawn, -most), most).astype(kind)


def setup_inputs(seed: int = 0) -> dict:
    splits = jax.random.split(jax.random.key(seed), 9)
    return {
        "queries": draw_queries(jax.random.fold_in(splits[8], 71), 0),
        "cached_keys": draw_cached_keys(jax.random.fold_in(splits[8], 71), 0),
        "cached_values": normal_values(splits[2], (TOKENS, KV_HEADS * HEAD_DIM), 1.0, 6.0, ((0, 64), (1, 8))),
        "fresh_keys": draw_fresh_keys(jax.random.fold_in(splits[8], 71), 0),
        "fresh_values": normal_values(splits[4], (ROWS, KV_HEADS * HEAD_DIM), 1.0, 6.0, ((0, 64), (1, 8))),
        "recompute_index": draw_recompute_index(jax.random.fold_in(splits[8], 71), 0),
        "recompute_count": uneven(splits[6], GROUPS, GROUPS * R_MAX * 7 // 8, R_MAX, 1).astype(jnp.int32),
        "group_offsets": draw_group_offsets(jax.random.fold_in(splits[8], 71), 0),
    }


def inverse_freq():
    half_dim = HEAD_DIM // 2
    exponent = jnp.arange(half_dim, dtype=jnp.float32) * 2.0 / HEAD_DIM
    base_freq = 1.0 / 500000.0 ** exponent
    wavelength = 2.0 * jnp.pi / base_freq
    smooth = (8192.0 / wavelength - 1.0) / 3.0
    blended_freq = (1.0 - smooth) * base_freq / 8.0 + smooth * base_freq
    return jnp.where(wavelength < 2048.0, base_freq, jnp.where(wavelength > 8192.0, base_freq / 8.0, blended_freq))

def rotate(values, positions):
    row_count = values.shape[0]
    head_count = values.shape[1] // HEAD_DIM
    half_dim = HEAD_DIM // 2
    angles = positions.astype(jnp.float32)[:, None] * inverse_freq()[None, :]
    cosine = jnp.cos(angles)[:, None, :]
    sine_part = jnp.sin(angles)[:, None, :]
    pieces_f = values.astype(jnp.float32).reshape(row_count, head_count, HEAD_DIM)
    first_half = pieces_f[:, :, :half_dim]
    second_half = pieces_f[:, :, half_dim:]
    turned = jnp.concatenate([first_half * cosine - second_half * sine_part, second_half * cosine + first_half * sine_part], axis=2)
    return turned.reshape(row_count, head_count * HEAD_DIM)

def reference(queries, cached_keys, cached_values, fresh_keys, fresh_values, recompute_index, recompute_count, group_offsets):
    heads_per = HEADS // KV_HEADS
    kv_width = KV_HEADS * HEAD_DIM
    positions = jnp.arange(GROUP_LEN, dtype=jnp.int32)
    slot_ids = jnp.arange(R_MAX, dtype=jnp.int32)
    score_scale = 1.0 / math.sqrt(HEAD_DIM)

    def join_group(number):
        start_pos = group_offsets[number]
        key_rows = lax.dynamic_slice_in_dim(cached_keys, (number * GROUP_LEN).astype(jnp.int32), GROUP_LEN, 0)
        value_rows = lax.dynamic_slice_in_dim(cached_values, (number * GROUP_LEN).astype(jnp.int32), GROUP_LEN, 0)
        fresh_key_rows = lax.dynamic_slice_in_dim(fresh_keys, (number * R_MAX).astype(jnp.int32), R_MAX, 0)
        fresh_value_rows = lax.dynamic_slice_in_dim(fresh_values, (number * R_MAX).astype(jnp.int32), R_MAX, 0)
        indices = recompute_index[number]
        live_rows = slot_ids < recompute_count[number]
        turned = rotate(key_rows, start_pos + 0 * positions).astype(jnp.bfloat16)
        fresh_turned = rotate(fresh_key_rows, start_pos + indices).astype(jnp.bfloat16)
        target = jnp.where(live_rows, indices, GROUP_LEN).astype(jnp.int32)
        blended_keys = turned.at[target].set(fresh_turned, mode='drop')
        blended_values = value_rows.at[target].set(fresh_value_rows, mode='drop')
        key_gap = fresh_turned.astype(jnp.float32) - turned[indices].astype(jnp.float32)
        value_gap = fresh_value_rows.astype(jnp.float32) - value_rows[indices].astype(jnp.float32)
        kv_drift = lax.optimization_barrier(jnp.sum(key_gap * key_gap + value_gap * value_gap, axis=1)) / (2.0 * KV_HEADS * HEAD_DIM)
        kv_drift = jnp.where(live_rows, kv_drift, jnp.zeros((), jnp.float32))
        return (blended_keys, blended_values, kv_drift)
    joined_keys, joined_values, drift = lax.map(join_group, jnp.arange(GROUPS, dtype=jnp.int32))
    joined_keys = joined_keys.reshape(TOKENS, kv_width)
    joined_values = joined_values.reshape(TOKENS, kv_width)
    query_pos = (group_offsets[:, None] + recompute_index).reshape(-1)
    turned_queries = rotate(queries, query_pos).astype(jnp.bfloat16)
    query_grid = turned_queries.reshape(GROUPS, R_MAX, KV_HEADS, heads_per, HEAD_DIM)
    key_pos = (group_offsets[:, None] + positions[None, :]).reshape(-1)
    key_grid = joined_keys.reshape(TOKENS, KV_HEADS, HEAD_DIM)
    value_grid = joined_values.reshape(TOKENS, KV_HEADS, HEAD_DIM)
    slot_pos = query_pos.reshape(GROUPS, R_MAX)

    def attend_pair(number):
        group_no = number // KV_HEADS
        kv_head = number % KV_HEADS
        picked = lax.dynamic_index_in_dim(query_grid, group_no, 0, keepdims=False)
        picked = lax.dynamic_index_in_dim(picked, kv_head, 1, keepdims=False).reshape(R_MAX * heads_per, HEAD_DIM)
        key_rows = lax.dynamic_index_in_dim(key_grid, kv_head, 1, keepdims=False)
        value_rows = lax.dynamic_index_in_dim(value_grid, kv_head, 1, keepdims=False)
        row_pos = jnp.repeat(lax.dynamic_index_in_dim(slot_pos, group_no, 0, keepdims=False), heads_per)
        scores = jnp.dot(picked, key_rows.T, preferred_element_type=jnp.float32) * score_scale
        visible = key_pos[None, :] <= row_pos[:, None]
        row_peak = lax.optimization_barrier(jnp.max(jnp.where(visible, scores, -jnp.inf), axis=1, keepdims=True))
        weights = jnp.where(visible, jnp.exp(scores - row_peak), jnp.zeros((), jnp.float32))
        denominator = lax.optimization_barrier(jnp.sum(weights, axis=1, keepdims=True))
        return jnp.dot(weights.astype(jnp.bfloat16), value_rows, preferred_element_type=jnp.float32) / denominator
    blended = lax.map(attend_pair, jnp.arange(GROUPS * KV_HEADS, dtype=jnp.int32))
    blended = blended.reshape(GROUPS, KV_HEADS, R_MAX, heads_per, HEAD_DIM).transpose(0, 2, 1, 3, 4).reshape(ROWS, HEADS * HEAD_DIM)
    live_all = (slot_ids[None, :] < recompute_count[:, None]).reshape(-1)
    attention = jnp.where(live_all[:, None], blended, jnp.zeros((), jnp.float32)).astype(jnp.bfloat16)
    return (attention, joined_keys, joined_values, drift)
```

```python
import functools
import math

import jax
import jax.numpy as jnp
from jax import lax
from jax.experimental import pallas as pl
from jax.experimental.pallas import tpu as pltpu
from jax.sharding import PartitionSpec as P

HEADS = 64
KV_HEADS = 8
HEAD_DIM = 128
HEADS_PER = HEADS // KV_HEADS
Z_HI, Y, CORES = 4, 8, 2
SLOTS = 48
GROUP_LEN = 320
ROWS = SLOTS * HEADS_PER
STAT_ROWS = 16
PAIR = CORES * GROUP_LEN
NEG_FILL = -1e30
EXP2_SCALE = math.log2(math.e) / math.sqrt(HEAD_DIM)
SCORE_SCALE = 1.0 / math.sqrt(HEAD_DIM)

VMEM = pl.BlockSpec(memory_space=pltpu.VMEM)
SMEM = pl.BlockSpec(memory_space=pltpu.SMEM)


def ctx_index(z_hi, y, core):
    return (z_hi * Y + y) * CORES + core


def mirrored(z_hi, y):
    return z_hi ^ ((Z_HI - 1) * (y & 1))


QUERY_GROUPS = [
    [ctx_index(mirrored(z, y), y, c) for y in range(Y)] for z in range(Z_HI) for c in range(CORES)
]
KEY_GROUPS = [[ctx_index(z, y, c) for z in range(Z_HI)] for y in range(Y) for c in range(CORES)]
CORE_SWAP = [(i, i ^ 1) for i in range(Z_HI * Y * CORES)]


def inverse_freq():
    half_dim = HEAD_DIM // 2
    exponent = jnp.arange(half_dim, dtype=jnp.float32) * 2.0 / HEAD_DIM
    base_freq = 1.0 / 500000.0**exponent
    wavelength = 2.0 * jnp.pi / base_freq
    smooth = (8192.0 / wavelength - 1.0) / 3.0
    blended_freq = (1.0 - smooth) * base_freq / 8.0 + smooth * base_freq
    return jnp.where(
        wavelength < 2048.0,
        base_freq,
        jnp.where(wavelength > 8192.0, base_freq / 8.0, blended_freq),
    )


def iota(shape, dim):
    return lax.broadcasted_iota(jnp.int32, shape, dim)


def column_of(row):
    n = row.shape[1]
    eye = iota((n, n), 0) == iota((n, n), 1)
    return jnp.sum(jnp.where(eye, jnp.broadcast_to(row, (n, n)), 0.0), axis=1, keepdims=True)


def row_of(wide):
    n = wide.shape[0]
    eye = iota((n, n), 0) == iota((n, n), 1)
    return jnp.sum(jnp.where(eye, wide, 0.0), axis=0, keepdims=True)


def prepare_kernel(
    offsets, count_ref, index_ref, freq_ref, q_ref, ck_ref, cv_ref, fk_ref, fv_ref,
    q_out, kv_out, jk_out, jv_out, drift_out,
):
    own_start = offsets[lax.axis_index("ctx")]
    count = count_ref[0]
    half = HEAD_DIM // 2
    index_row = index_ref[...]
    index_col = column_of(index_row.astype(jnp.float32))
    freq = freq_ref[...]
    start_row = jnp.full((1, HEAD_DIM), own_start, jnp.int32).astype(jnp.float32)
    slot_angle = (index_col + start_row[:, :1]) * freq
    group_angle = start_row * freq
    sign = jnp.where(iota((1, HEAD_DIM), 1) < half, -1.0, 1.0)
    slot_cos, slot_sin = jnp.cos(slot_angle), jnp.sin(slot_angle) * sign
    group_cos, group_sin = jnp.cos(group_angle), jnp.sin(group_angle) * sign

    def turn(rows, cosine, sine):
        x = rows.astype(jnp.float32)
        return (x * cosine + pltpu.roll(x, half, 1) * sine).astype(jnp.bfloat16)

    for h in range(HEADS_PER):
        head = turn(q_ref[:, h * HEAD_DIM : (h + 1) * HEAD_DIM], slot_cos, slot_sin)
        for y in range(Y):
            q_out[y, h * SLOTS : (h + 1) * SLOTS, :] = head

    turned = turn(ck_ref[...], group_cos, group_sin)
    fresh = turn(fk_ref[...], slot_cos, slot_sin)
    cached_values = cv_ref[...]
    fresh_values = fv_ref[...]

    live = iota((1, SLOTS), 1) < count
    chosen = jnp.where(live, index_row, -1)
    picker = jnp.where(iota((GROUP_LEN, SLOTS), 0) == chosen, 1.0, 0.0)
    covered = jnp.sum(picker, axis=1, keepdims=True) > 0.0
    picker = picker.astype(jnp.bfloat16)
    joined_keys = jnp.where(
        covered,
        jnp.dot(picker, fresh, preferred_element_type=jnp.float32),
        turned.astype(jnp.float32),
    ).astype(jnp.bfloat16)
    joined_values = jnp.where(
        covered,
        jnp.dot(picker, fresh_values, preferred_element_type=jnp.float32),
        cached_values.astype(jnp.float32),
    ).astype(jnp.bfloat16)
    jk_out[...] = joined_keys
    jv_out[...] = joined_values
    kv_out[:, :HEAD_DIM] = joined_keys
    kv_out[:, HEAD_DIM:] = joined_values

    reader = jnp.where(
        iota((SLOTS, GROUP_LEN), 1).astype(jnp.float32) == index_col, 1.0, 0.0
    ).astype(jnp.bfloat16)
    key_gap = fresh.astype(jnp.float32) - jnp.dot(
        reader, turned, preferred_element_type=jnp.float32
    )
    value_gap = fresh_values.astype(jnp.float32) - jnp.dot(
        reader, cached_values, preferred_element_type=jnp.float32
    )
    squares = jnp.sum(key_gap * key_gap + value_gap * value_gap, axis=1, keepdims=True)
    drift_row = row_of(jnp.broadcast_to(squares, (SLOTS, SLOTS)))
    for h in range(KV_HEADS):
        drift_out[h] = drift_row


def attend_kernel(index_ref, q_ref, own_ref, other_ref, out_ref, keys, values, scores, peaks):
    me = lax.axis_index("ctx")
    core = lax.rem(me, CORES)
    y_own = lax.rem(me // CORES, Y)
    z_own = me // (CORES * Y)
    z_group = jnp.where(lax.rem(y_own, 2) == 1, Z_HI - 1 - z_own, z_own)

    ones = jnp.ones((GROUP_LEN, HEAD_DIM), jnp.bfloat16)
    for z in range(Z_HI):
        for part, ref in enumerate((own_ref, other_ref)):
            source = slice(z * GROUP_LEN, (z + 1) * GROUP_LEN)
            target = slice(part * GROUP_LEN, (part + 1) * GROUP_LEN)
            keys[z, target, :] = ref[source, :HEAD_DIM]
            values[z, target, :HEAD_DIM] = ref[source, HEAD_DIM:]
            values[z, target, HEAD_DIM:] = ones

    def score(queries, block):
        return lax.dot_general(
            queries, keys[block], (((1,), (1,)), ((), ())), preferred_element_type=jnp.float32
        )

    def note(block, found):
        scores[block] = found
        top = found[:, :HEAD_DIM]
        for at in range(HEAD_DIM, PAIR, HEAD_DIM):
            top = jnp.maximum(top, found[:, at : at + HEAD_DIM])
        peaks[...] = jnp.maximum(peaks[...], top)

    def one_group(y, carry):
        z_query = jnp.where(lax.rem(y, 2) == 1, Z_HI - 1 - z_group, z_group)
        whole = z_query + jnp.where(y_own < y, 1, 0)
        queries = q_ref[y]
        peaks[...] = jnp.full((ROWS, HEAD_DIM), NEG_FILL, jnp.float32)

        def full(block, inner):
            note(block, score(queries, block))
            return inner

        lax.fori_loop(0, whole, full, 0)

        @pl.when(y == y_own)
        def _():
            found = score(queries, whole)
            index_col = column_of(index_ref[...].astype(jnp.float32))
            reach = jnp.concatenate([index_col] * HEADS_PER, axis=0)
            token = iota((1, PAIR), 1)
            place = jnp.where(
                token < GROUP_LEN, token, jnp.where(core == 1, -1, 2 * GROUP_LEN)
            ).astype(jnp.float32)
            note(whole, jnp.where(place <= reach, found, NEG_FILL))

        blocks = whole + jnp.where(y == y_own, 1, 0)
        peak = jnp.max(peaks[...], axis=1, keepdims=True)

        def weigh(block, total):
            weights = jnp.exp2((scores[block] - peak) * EXP2_SCALE).astype(jnp.bfloat16)
            return total + jnp.dot(weights, values[block], preferred_element_type=jnp.float32)

        total = lax.fori_loop(
            0, blocks, weigh, jnp.zeros((ROWS, 2 * HEAD_DIM), jnp.float32)
        )
        mass = total[:, HEAD_DIM:]
        seen = mass > 0.0
        safe = jnp.where(seen, mass, 1.0)
        out_ref[y, :ROWS, :] = (total[:, :HEAD_DIM] / safe).astype(jnp.bfloat16)
        level = jnp.where(seen, peak * SCORE_SCALE + jnp.log(safe), NEG_FILL)
        stat = jnp.zeros((STAT_ROWS, HEAD_DIM), jnp.float32)
        row = iota((STAT_ROWS, HEAD_DIM), 0)
        for k in range(ROWS // HEAD_DIM):
            rest = row_of(level[k * HEAD_DIM : (k + 1) * HEAD_DIM])
            for piece in range(3):
                part = rest.astype(jnp.bfloat16).astype(jnp.float32)
                stat = jnp.where(row == 3 * piece + k, part, stat)
                rest = rest - part
        out_ref[y, ROWS:, :] = stat.astype(jnp.bfloat16)
        return carry

    lax.fori_loop(0, Y, one_group, 0)


def merge_kernel(count_ref, parts_ref, out_ref):
    live = iota((SLOTS, HEAD_DIM), 0) < count_ref[0]
    eye = iota((HEAD_DIM, HEAD_DIM), 0) == iota((HEAD_DIM, HEAD_DIM), 1)
    stats = [parts_ref[y, ROWS:, :].astype(jnp.float32) for y in range(Y)]
    merged = []
    for k in range(ROWS // HEAD_DIM):
        levels = [s[k : k + 1] + s[k + 3 : k + 4] + s[k + 6 : k + 7] for s in stats]
        top = functools.reduce(jnp.maximum, levels)
        shares = [jnp.exp(level - top) for level in levels]
        whole = functools.reduce(jnp.add, shares)
        total = jnp.zeros((HEAD_DIM, HEAD_DIM), jnp.float32)
        for y in range(Y):
            share = jnp.broadcast_to(shares[y] / whole, (HEAD_DIM, HEAD_DIM))
            share = jnp.sum(jnp.where(eye, share, 0.0), axis=1, keepdims=True)
            part = parts_ref[y, k * HEAD_DIM : (k + 1) * HEAD_DIM, :].astype(jnp.float32)
            total = total + share * part
        merged.append(total)
    merged = jnp.concatenate(merged, axis=0)
    for h in range(HEADS_PER):
        head = jnp.where(live, merged[h * SLOTS : (h + 1) * SLOTS], 0.0)
        out_ref[:, h * HEAD_DIM : (h + 1) * HEAD_DIM] = head.astype(jnp.bfloat16)


def kernel_params(mib):
    return pltpu.CompilerParams(vmem_limit_bytes=mib << 20)


def shards(
    queries,
    cached_keys,
    cached_values,
    fresh_keys,
    fresh_values,
    recompute_index,
    recompute_count,
    group_offsets,
):
    bf16, f32 = jnp.bfloat16, jnp.float32
    shape = jax.ShapeDtypeStruct
    freq = inverse_freq()
    freq = jnp.concatenate([freq, freq])[None, :]
    copies, own_kv, joined_keys, joined_values, squares = pl.pallas_call(
        prepare_kernel,
        out_shape=(
            shape((Y, ROWS, HEAD_DIM), bf16),
            shape((GROUP_LEN, 2 * HEAD_DIM), bf16),
            shape((GROUP_LEN, HEAD_DIM), bf16),
            shape((GROUP_LEN, HEAD_DIM), bf16),
            shape((KV_HEADS, 1, SLOTS), f32),
        ),
        in_specs=[SMEM, SMEM] + [VMEM] * 7,
        out_specs=[VMEM] * 5,
        compiler_params=kernel_params(16),
        name="prepare",
    )(
        group_offsets, recompute_count, recompute_index, freq,
        queries, cached_keys, cached_values, fresh_keys, fresh_values,
    )

    all_queries = lax.all_to_all(
        copies, "ctx", 0, 0, axis_index_groups=QUERY_GROUPS, tiled=True
    )
    core_kv = lax.all_gather(own_kv, "ctx", axis=0, axis_index_groups=KEY_GROUPS, tiled=True)
    other_kv = lax.ppermute(core_kv, "ctx", CORE_SWAP)

    partial = pl.pallas_call(
        attend_kernel,
        out_shape=shape((Y, ROWS + STAT_ROWS, HEAD_DIM), bf16),
        in_specs=[VMEM] * 4,
        out_specs=VMEM,
        scratch_shapes=[
            pltpu.VMEM((Z_HI, PAIR, HEAD_DIM), bf16),
            pltpu.VMEM((Z_HI, PAIR, 2 * HEAD_DIM), bf16),
            pltpu.VMEM((Z_HI, ROWS, PAIR), f32),
            pltpu.VMEM((ROWS, HEAD_DIM), f32),
        ],
        compiler_params=kernel_params(28),
        name="attend",
    )(recompute_index, all_queries, core_kv, other_kv)

    squares, partial = lax.optimization_barrier((squares, partial))
    parts = lax.all_to_all(partial, "ctx", 0, 0, axis_index_groups=QUERY_GROUPS, tiled=True)
    drift = lax.all_to_all(squares, "head", 0, 0, tiled=True).sum(axis=0)
    drift = drift / (2.0 * KV_HEADS * HEAD_DIM)
    drift = jnp.where(iota((1, SLOTS), 1) < recompute_count[0], drift, 0.0)

    attention = pl.pallas_call(
        merge_kernel,
        out_shape=shape((SLOTS, HEADS_PER * HEAD_DIM), bf16),
        in_specs=[SMEM, VMEM],
        out_specs=VMEM,
        compiler_params=kernel_params(16),
        name="merge",
    )(recompute_count, parts)
    return (attention, joined_keys, joined_values, drift)


def solution(mesh):
    return jax.shard_map(
        shards,
        mesh=mesh,
        in_specs=(
            P("ctx", "head"),
            P("ctx", "head"),
            P("ctx", "head"),
            P("ctx", "head"),
            P("ctx", "head"),
            P("ctx", None),
            P("ctx"),
            P(),
        ),
        out_specs=(P("ctx", "head"), P("ctx", "head"), P("ctx", "head"), P("ctx", None)),
        check_vma=False,
    )
```

```python
import functools
import math

import jax
import jax.numpy as jnp
from jax import lax
from jax.experimental import pallas as pl
from jax.experimental.pallas import tpu as pltpu
from jax.sharding import PartitionSpec as P


HEADS = 64
KV_HEADS = 8
HEAD_DIM = 128
HEADS_PER = HEADS // KV_HEADS
Z_HI, Y, CORES = 4, 8, 2
SLOTS = 48
GROUP_LEN = 320
ROWS = SLOTS * HEADS_PER
STAT_ROWS = 16
PAIR = CORES * GROUP_LEN
NEG_FILL = -1e30
EXP2_SCALE = math.log2(math.e) / math.sqrt(HEAD_DIM)
SCORE_SCALE = 1.0 / math.sqrt(HEAD_DIM)

VMEM = pl.BlockSpec(memory_space=pltpu.VMEM)
SMEM = pl.BlockSpec(memory_space=pltpu.SMEM)
HBM = pl.BlockSpec(memory_space=pltpu.HBM)


def ctx_index(z_hi, y, core):
    return (z_hi * Y + y) * CORES + core


QUERY_GROUPS = [[ctx_index(z, y, c) for y in range(Y)] for z in range(Z_HI) for c in range(CORES)]
KEY_GROUPS = [[ctx_index(z, y, c) for z in range(Z_HI)] for y in range(Y) for c in range(CORES)]
CORE_SWAP = [(i, i ^ 1) for i in range(Z_HI * Y * CORES)]


def inverse_freq():
    half_dim = HEAD_DIM // 2
    exponent = jnp.arange(half_dim, dtype=jnp.float32) * 2.0 / HEAD_DIM
    base_freq = 1.0 / 500000.0**exponent
    wavelength = 2.0 * jnp.pi / base_freq
    smooth = (8192.0 / wavelength - 1.0) / 3.0
    blended_freq = (1.0 - smooth) * base_freq / 8.0 + smooth * base_freq
    return jnp.where(
        wavelength < 2048.0,
        base_freq,
        jnp.where(wavelength > 8192.0, base_freq / 8.0, blended_freq),
    )


def iota(shape, dim):
    return lax.broadcasted_iota(jnp.int32, shape, dim)


def column_of(row):
    n = row.shape[1]
    eye = iota((n, n), 0) == iota((n, n), 1)
    return jnp.sum(jnp.where(eye, jnp.broadcast_to(row, (n, n)), 0.0), axis=1, keepdims=True)


def row_of(wide):
    n = wide.shape[0]
    eye = iota((n, n), 0) == iota((n, n), 1)
    return jnp.sum(jnp.where(eye, wide, 0.0), axis=0, keepdims=True)


def prepare_kernel(
    offsets, count_ref, freq_ref, index_hbm, q_hbm, ck_hbm, cv_hbm, fk_hbm, fv_hbm,
    q_out, kv_out, jk_out, jv_out, drift_out,
    index_ref, q_ref, ck_ref, cv_ref, fk_ref, fv_ref, arrived,
):
    copies = [
        pltpu.make_async_copy(source, target, arrived.at[i])
        for i, (source, target) in enumerate((
            (index_hbm, index_ref), (q_hbm, q_ref), (fk_hbm, fk_ref),
            (ck_hbm, ck_ref), (fv_hbm, fv_ref), (cv_hbm, cv_ref),
        ))
    ]
    for copy in copies:
        copy.start()
    copies[0].wait()
    own_start = offsets[lax.axis_index("ctx")]
    count = count_ref[0]
    half = HEAD_DIM // 2
    index_row = index_ref[...]
    index_col = column_of(index_row.astype(jnp.float32))
    freq = freq_ref[...]
    start_row = jnp.full((1, HEAD_DIM), own_start, jnp.int32).astype(jnp.float32)
    slot_angle = (index_col + start_row[:, :1]) * freq
    group_angle = start_row * freq
    sign = jnp.where(iota((1, HEAD_DIM), 1) < half, -1.0, 1.0)
    slot_cos, slot_sin = jnp.cos(slot_angle), jnp.sin(slot_angle) * sign
    group_cos, group_sin = jnp.cos(group_angle), jnp.sin(group_angle) * sign

    def turn(rows, cosine, sine):
        x = rows.astype(jnp.float32)
        return (x * cosine + pltpu.roll(x, half, 1) * sine).astype(jnp.bfloat16)

    for copy in copies[1:]:
        copy.wait()
    for h in range(HEADS_PER):
        head = turn(q_ref[:, h * HEAD_DIM : (h + 1) * HEAD_DIM], slot_cos, slot_sin)
        for y in range(Y):
            q_out[y, h * SLOTS : (h + 1) * SLOTS, :] = head

    turned = turn(ck_ref[...], group_cos, group_sin)
    fresh = turn(fk_ref[...], slot_cos, slot_sin)
    cached_values = cv_ref[...]
    fresh_values = fv_ref[...]

    live = iota((1, SLOTS), 1) < count
    chosen = jnp.where(live, index_row, -1)
    picker = jnp.where(iota((GROUP_LEN, SLOTS), 0) == chosen, 1.0, 0.0)
    covered = jnp.sum(picker, axis=1, keepdims=True) > 0.0
    picker = picker.astype(jnp.bfloat16)
    joined_keys = jnp.where(
        covered,
        jnp.dot(picker, fresh, preferred_element_type=jnp.float32),
        turned.astype(jnp.float32),
    ).astype(jnp.bfloat16)
    joined_values = jnp.where(
        covered,
        jnp.dot(picker, fresh_values, preferred_element_type=jnp.float32),
        cached_values.astype(jnp.float32),
    ).astype(jnp.bfloat16)
    jk_out[...] = joined_keys
    jv_out[...] = joined_values
    kv_out[:, :HEAD_DIM] = joined_keys
    kv_out[:, HEAD_DIM:] = joined_values

    reader = jnp.where(
        iota((SLOTS, GROUP_LEN), 1).astype(jnp.float32) == index_col, 1.0, 0.0
    ).astype(jnp.bfloat16)
    key_gap = fresh.astype(jnp.float32) - jnp.dot(
        reader, turned, preferred_element_type=jnp.float32
    )
    value_gap = fresh_values.astype(jnp.float32) - jnp.dot(
        reader, cached_values, preferred_element_type=jnp.float32
    )
    squares = jnp.sum(key_gap * key_gap + value_gap * value_gap, axis=1, keepdims=True)
    drift_row = row_of(jnp.broadcast_to(squares, (SLOTS, SLOTS)))
    drift_out[...] = drift_row


def attend_kernel(
    index_ref, q_ref, own_ref, other_ref, out_ref, keys, values, reach_ref,
    scores_even, scores_odd, peaks_even, peaks_odd,
):
    me = lax.axis_index("ctx")
    core = lax.rem(me, CORES)
    y_own = lax.rem(me // CORES, Y)
    z_own = me // (CORES * Y)

    ones = jnp.ones((GROUP_LEN, HEAD_DIM), jnp.bfloat16)
    for z in range(Z_HI):
        for part, ref in enumerate((own_ref, other_ref)):
            source = slice(z * GROUP_LEN, (z + 1) * GROUP_LEN)
            target = slice(z * PAIR + part * GROUP_LEN, z * PAIR + (part + 1) * GROUP_LEN)
            keys[target, :] = ref[source, :HEAD_DIM]
            values[target, :HEAD_DIM] = ref[source, HEAD_DIM:]
            values[target, HEAD_DIM:] = ones

    token = iota((1, PAIR), 1)
    place = jnp.where(
        token < GROUP_LEN, token, jnp.where(core == 1, -1, GROUP_LEN)
    ).astype(jnp.float32)
    index_col = column_of(index_ref[...].astype(jnp.float32))
    reach_ref[...] = jnp.broadcast_to(
        jnp.concatenate([index_col] * HEADS_PER, axis=0), (ROWS, HEAD_DIM)
    )

    def score(y, blocks, masked, scores, peaks):
        queries = q_ref[y]
        reach = jnp.where(
            y == y_own, reach_ref[...], jnp.where(y_own < y, 2.0 * GROUP_LEN, -2.0)
        )
        top = None
        for block in range(blocks):
            found = lax.dot_general(
                queries,
                keys[block * PAIR : (block + 1) * PAIR, :],
                (((1,), (1,)), ((), ())),
                preferred_element_type=jnp.float32,
            )
            limit = None
            if block in masked:
                limit = jnp.where(
                    z_own == block, reach, jnp.where(block < z_own, 2.0 * GROUP_LEN, -2.0)
                )
            for at in range(0, PAIR, HEAD_DIM):
                part = found[:, at : at + HEAD_DIM]
                if limit is not None:
                    part = jnp.where(place[:, at : at + HEAD_DIM] <= limit, part, NEG_FILL)
                scores[:, block * PAIR + at : block * PAIR + at + HEAD_DIM] = part
                top = part if top is None else jnp.maximum(top, part)
        peaks[...] = jnp.broadcast_to(jnp.max(top, axis=1, keepdims=True), (ROWS, HEAD_DIM))

    def weigh(y, blocks, scores, peaks):
        peak = peaks[...]
        size = blocks * PAIR
        weights = [
            jnp.exp2((scores[:, at : at + HEAD_DIM] - peak) * EXP2_SCALE).astype(jnp.bfloat16)
            for at in range(0, size, HEAD_DIM)
        ]
        total = jnp.dot(
            jnp.concatenate(weights, axis=1), values[:size, :], preferred_element_type=jnp.float32
        )
        mass = total[:, HEAD_DIM:]
        out_ref[y, :ROWS, :] = (total[:, :HEAD_DIM] / mass).astype(jnp.bfloat16)
        level = jnp.where(peak > 0.5 * NEG_FILL, peak * SCORE_SCALE + jnp.log(mass), NEG_FILL)
        stat = jnp.zeros((STAT_ROWS, HEAD_DIM), jnp.float32)
        row = iota((STAT_ROWS, HEAD_DIM), 0)
        for k in range(ROWS // HEAD_DIM):
            rest = row_of(level[k * HEAD_DIM : (k + 1) * HEAD_DIM])
            for piece in range(3):
                part = rest.astype(jnp.bfloat16).astype(jnp.float32)
                stat = jnp.where(row == 3 * piece + k, part, stat)
                rest = rest - part
        out_ref[y, ROWS:, :] = stat.astype(jnp.bfloat16)

    def all_groups(blocks, masked):
        even, odd = (scores_even, peaks_even), (scores_odd, peaks_odd)
        score(0, blocks, masked, *even)

        def step(pair, carry):
            y = 2 * pair
            score(y + 1, blocks, masked, *odd)
            weigh(y, blocks, *even)
            score(jnp.minimum(y + 2, Y - 1), blocks, masked, *even)
            weigh(y + 1, blocks, *odd)
            return carry

        lax.fori_loop(0, Y // 2, step, 0)

    @pl.when(z_own == Z_HI - 1)
    def _():
        all_groups(Z_HI, (Z_HI - 1,))

    @pl.when(z_own != Z_HI - 1)
    def _():
        all_groups(Z_HI - 1, tuple(range(Z_HI - 1)))


def merge_kernel(count_ref, parts_ref, out_ref):
    live = iota((SLOTS, HEAD_DIM), 0) < count_ref[0]
    eye = iota((HEAD_DIM, HEAD_DIM), 0) == iota((HEAD_DIM, HEAD_DIM), 1)
    stats = [parts_ref[y, ROWS:, :].astype(jnp.float32) for y in range(Y)]
    merged = []
    for k in range(ROWS // HEAD_DIM):
        levels = [s[k : k + 1] + s[k + 3 : k + 4] + s[k + 6 : k + 7] for s in stats]
        top = functools.reduce(jnp.maximum, levels)
        shares = [jnp.exp(level - top) for level in levels]
        whole = functools.reduce(jnp.add, shares)
        total = jnp.zeros((HEAD_DIM, HEAD_DIM), jnp.float32)
        for y in range(Y):
            share = jnp.broadcast_to(shares[y] / whole, (HEAD_DIM, HEAD_DIM))
            share = jnp.sum(jnp.where(eye, share, 0.0), axis=1, keepdims=True)
            part = parts_ref[y, k * HEAD_DIM : (k + 1) * HEAD_DIM, :].astype(jnp.float32)
            total = total + share * part
        merged.append(total)
    merged = jnp.concatenate(merged, axis=0)
    for h in range(HEADS_PER):
        head = jnp.where(live, merged[h * SLOTS : (h + 1) * SLOTS], 0.0)
        out_ref[:, h * HEAD_DIM : (h + 1) * HEAD_DIM] = head.astype(jnp.bfloat16)


def kernel_params(mib):
    return pltpu.CompilerParams(vmem_limit_bytes=mib << 20)


def shards(
    queries,
    cached_keys,
    cached_values,
    fresh_keys,
    fresh_values,
    recompute_index,
    recompute_count,
    group_offsets,
):
    bf16, f32 = jnp.bfloat16, jnp.float32
    shape = jax.ShapeDtypeStruct
    freq = inverse_freq()
    freq = jnp.concatenate([freq, freq])[None, :]
    copies, own_kv, joined_keys, joined_values, squares = pl.pallas_call(
        prepare_kernel,
        out_shape=(
            shape((Y, ROWS, HEAD_DIM), bf16),
            shape((GROUP_LEN, 2 * HEAD_DIM), bf16),
            shape((GROUP_LEN, HEAD_DIM), bf16),
            shape((GROUP_LEN, HEAD_DIM), bf16),
            shape((1, SLOTS), f32),
        ),
        in_specs=[SMEM, SMEM, VMEM] + [HBM] * 6,
        out_specs=[VMEM] * 5,
        scratch_shapes=[
            pltpu.VMEM((1, SLOTS), jnp.int32),
            pltpu.VMEM((SLOTS, HEADS_PER * HEAD_DIM), bf16),
            pltpu.VMEM((GROUP_LEN, HEAD_DIM), bf16),
            pltpu.VMEM((GROUP_LEN, HEAD_DIM), bf16),
            pltpu.VMEM((SLOTS, HEAD_DIM), bf16),
            pltpu.VMEM((SLOTS, HEAD_DIM), bf16),
            pltpu.SemaphoreType.DMA((6,)),
        ],
        name="prepare",
    )(
        group_offsets, recompute_count, freq, recompute_index,
        queries, cached_keys, cached_values, fresh_keys, fresh_values,
    )

    all_queries = lax.all_to_all(
        copies, "ctx", 0, 0, axis_index_groups=QUERY_GROUPS, tiled=True
    )
    core_kv = lax.all_gather(own_kv, "ctx", axis=0, axis_index_groups=KEY_GROUPS, tiled=True)
    other_kv = lax.ppermute(core_kv, "ctx", CORE_SWAP)

    partial = pl.pallas_call(
        attend_kernel,
        out_shape=shape((Y, ROWS + STAT_ROWS, HEAD_DIM), bf16),
        in_specs=[VMEM] * 4,
        out_specs=VMEM,
        scratch_shapes=[
            pltpu.VMEM((Z_HI * PAIR, HEAD_DIM), bf16),
            pltpu.VMEM((Z_HI * PAIR, 2 * HEAD_DIM), bf16),
            pltpu.VMEM((ROWS, HEAD_DIM), f32),
            pltpu.VMEM((ROWS, Z_HI * PAIR), f32),
            pltpu.VMEM((ROWS, Z_HI * PAIR), f32),
            pltpu.VMEM((ROWS, HEAD_DIM), f32),
            pltpu.VMEM((ROWS, HEAD_DIM), f32),
        ],
        compiler_params=kernel_params(28),
        name="attend",
    )(recompute_index, all_queries, core_kv, other_kv)

    parts = lax.all_to_all(
        partial, "ctx", 0, 0, axis_index_groups=QUERY_GROUPS, tiled=True
    )
    squares = lax.all_gather(squares, "head", axis=0, tiled=True)
    drift = squares.sum(axis=0, keepdims=True)
    drift = drift / (2.0 * KV_HEADS * HEAD_DIM)
    drift = jnp.where(iota((1, SLOTS), 1) < recompute_count[0], drift, 0.0)

    attention = pl.pallas_call(
        merge_kernel,
        out_shape=shape((SLOTS, HEADS_PER * HEAD_DIM), bf16),
        in_specs=[SMEM, VMEM],
        out_specs=VMEM,
        compiler_params=kernel_params(16),
        name="merge",
    )(recompute_count, parts)
    return (attention, joined_keys, joined_values, drift)


def solution(mesh):
    return jax.shard_map(
        shards,
        mesh=mesh,
        in_specs=(
            P("ctx", "head"),
            P("ctx", "head"),
            P("ctx", "head"),
            P("ctx", "head"),
            P("ctx", "head"),
            P("ctx", None),
            P("ctx"),
            P(),
        ),
        out_specs=(P("ctx", "head"), P("ctx", "head"), P("ctx", "head"), P("ctx", None)),
        check_vma=False,
    )
```

```python
import functools
import math

import jax
import jax.numpy as jnp
from jax import lax
from jax.experimental import pallas as pl
from jax.experimental.pallas import tpu as pltpu
from jax.sharding import PartitionSpec as P


HEADS = 64
KV_HEADS = 8
HEAD_DIM = 128
HEADS_PER = HEADS // KV_HEADS
Z_HI, Y, CORES = 4, 8, 2
SLOTS = 48
GROUP_LEN = 320
ROWS = SLOTS * HEADS_PER
STAT_ROWS = 8
ONES = 16
STEP = 256
CHUNK = 256
WIDE = 64
SHORT = 1024
NEG_FILL = -1e30
EXP2_SCALE = math.log2(math.e) / math.sqrt(HEAD_DIM)
SCORE_SCALE = 1.0 / math.sqrt(HEAD_DIM)

VMEM = pl.BlockSpec(memory_space=pltpu.VMEM)
SMEM = pl.BlockSpec(memory_space=pltpu.SMEM)
HBM = pl.BlockSpec(memory_space=pltpu.HBM)


def ctx_index(z_hi, y, core):
    return (z_hi * Y + y) * CORES + core


QUERY_GROUPS = [[ctx_index(z, y, c) for y in range(Y)] for z in range(Z_HI) for c in range(CORES)]
KEY_GROUPS = [[ctx_index(z, y, c) for z in range(Z_HI)] for y in range(Y) for c in range(CORES)]
CORE_SWAP = [(i, i ^ 1) for i in range(Z_HI * Y * CORES)]


def inverse_freq():
    half_dim = HEAD_DIM // 2
    exponent = jnp.arange(half_dim, dtype=jnp.float32) * 2.0 / HEAD_DIM
    base_freq = 1.0 / 500000.0**exponent
    wavelength = 2.0 * jnp.pi / base_freq
    smooth = (8192.0 / wavelength - 1.0) / 3.0
    blended_freq = (1.0 - smooth) * base_freq / 8.0 + smooth * base_freq
    return jnp.where(
        wavelength < 2048.0,
        base_freq,
        jnp.where(wavelength > 8192.0, base_freq / 8.0, blended_freq),
    )


def iota(shape, dim):
    return lax.broadcasted_iota(jnp.int32, shape, dim)


def column_of(row):
    n = row.shape[1]
    eye = iota((n, n), 0) == iota((n, n), 1)
    return jnp.sum(jnp.where(eye, jnp.broadcast_to(row, (n, n)), 0.0), axis=1, keepdims=True)


def row_of(wide):
    n = wide.shape[0]
    eye = iota((n, n), 0) == iota((n, n), 1)
    return jnp.sum(jnp.where(eye, wide, 0.0), axis=0, keepdims=True)


def prepare_kernel(
    offsets, count_ref, freq_ref, index_hbm, q_hbm, ck_hbm, cv_hbm, fk_hbm, fv_hbm,
    q_out, kv_out, jk_out, jv_out, drift_out,
    index_ref, q_ref, ck_ref, cv_ref, fk_ref, fv_ref, turned_q, arrived, left,
):
    copies = [
        pltpu.make_async_copy(source, target, arrived.at[i])
        for i, (source, target) in enumerate((
            (index_hbm, index_ref), (q_hbm, q_ref), (fk_hbm, fk_ref),
            (ck_hbm, ck_ref), (fv_hbm, fv_ref), (cv_hbm, cv_ref),
        ))
    ]
    for copy in copies:
        copy.start()
    copies[0].wait()
    own_start = offsets[lax.axis_index("ctx")]
    count = count_ref[0]
    half = HEAD_DIM // 2
    index_row = index_ref[...]
    index_col = column_of(index_row.astype(jnp.float32))
    freq = freq_ref[...]
    start_row = jnp.full((1, HEAD_DIM), own_start, jnp.int32).astype(jnp.float32)
    slot_angle = (index_col + start_row[:, :1]) * freq
    group_angle = start_row * freq
    sign = jnp.where(iota((1, HEAD_DIM), 1) < half, -1.0, 1.0)
    slot_cos, slot_sin = jnp.cos(slot_angle), jnp.sin(slot_angle) * sign
    group_cos, group_sin = jnp.cos(group_angle), jnp.sin(group_angle) * sign

    def turn(rows, cosine, sine):
        x = rows.astype(jnp.float32)
        return (x * cosine + pltpu.roll(x, half, 1) * sine).astype(jnp.bfloat16)

    copies[1].wait()
    for h in range(HEADS_PER):
        head = turn(q_ref[:, h * HEAD_DIM : (h + 1) * HEAD_DIM], slot_cos, slot_sin)
        turned_q[h * SLOTS : (h + 1) * SLOTS, :] = head
    sends = [pltpu.make_async_copy(turned_q, q_out.at[y], left.at[y]) for y in range(Y)]
    for send in sends:
        send.start()

    for copy in copies[2:]:
        copy.wait()
    turned = turn(ck_ref[...], group_cos, group_sin)
    fresh = turn(fk_ref[...], slot_cos, slot_sin)
    cached_values = cv_ref[...]
    fresh_values = fv_ref[...]

    live = iota((1, SLOTS), 1) < count
    chosen = jnp.where(live, index_row, -1)
    picker = jnp.where(iota((GROUP_LEN, SLOTS), 0) == chosen, 1.0, 0.0)
    covered = jnp.sum(picker, axis=1, keepdims=True) > 0.0
    picker = picker.astype(jnp.bfloat16)
    joined_keys = jnp.where(
        covered,
        jnp.dot(picker, fresh, preferred_element_type=jnp.float32),
        turned.astype(jnp.float32),
    ).astype(jnp.bfloat16)
    joined_values = jnp.where(
        covered,
        jnp.dot(picker, fresh_values, preferred_element_type=jnp.float32),
        cached_values.astype(jnp.float32),
    ).astype(jnp.bfloat16)
    jk_out[...] = joined_keys
    jv_out[...] = joined_values
    kv_out[:, :HEAD_DIM] = joined_keys
    kv_out[:, HEAD_DIM:] = joined_values

    reader = jnp.where(
        iota((SLOTS, GROUP_LEN), 1).astype(jnp.float32) == index_col, 1.0, 0.0
    ).astype(jnp.bfloat16)
    key_gap = fresh.astype(jnp.float32) - jnp.dot(
        reader, turned, preferred_element_type=jnp.float32
    )
    value_gap = fresh_values.astype(jnp.float32) - jnp.dot(
        reader, cached_values, preferred_element_type=jnp.float32
    )
    squares = jnp.sum(key_gap * key_gap + value_gap * value_gap, axis=1, keepdims=True)
    drift_row = row_of(jnp.broadcast_to(squares, (SLOTS, SLOTS)))
    drift_out[...] = drift_row
    for send in sends:
        send.wait()


def attend_kernel(
    index_ref, q_ref, own_ref, other_ref, out_ref, values, own_limit, other_limit,
    scores_even, scores_odd, peaks_even, peaks_odd,
):
    me = lax.axis_index("ctx")
    core = lax.rem(me, CORES)
    y_own = lax.rem(me // CORES, Y)
    z_own = me // (CORES * Y)
    gathered = Z_HI * GROUP_LEN
    sources = (own_ref, own_limit), (other_ref, other_limit)

    index_col = column_of(index_ref[...].astype(jnp.float32))
    slot = lax.rem(iota((SLOTS, ROWS), 1), SLOTS)
    own_index = jnp.sum(
        jnp.where(slot == iota((SLOTS, ROWS), 0), index_col, 0.0), axis=0, keepdims=True
    )
    before = z_own * GROUP_LEN - 1
    full = before + GROUP_LEN
    for y in range(Y):
        lanes = slice(y * ROWS, (y + 1) * ROWS)
        beside = jnp.where(y_own < y, full, before)
        own_limit[:, lanes] = jnp.where(
            y == y_own, own_index.astype(jnp.int32) + (before + 1), beside
        )
        other_limit[:, lanes] = jnp.full(
            (1, ROWS), jnp.where(jnp.logical_and(y == y_own, core == 1), full, beside), jnp.int32
        )

    def score(step, size, masked, scores, peaks):
        lanes = pl.ds(pl.multiple_of(step * STEP, STEP), STEP)
        queries = q_ref[lanes, :]
        top = None
        for part, (source, limit_ref) in enumerate(sources):
            limit = limit_ref[:, lanes]
            for at in range(0, size, CHUNK):
                found = lax.dot_general(
                    source[at : at + CHUNK, :HEAD_DIM],
                    queries,
                    (((1,), (1,)), ((), ())),
                    preferred_element_type=jnp.float32,
                )
                if at + CHUNK > masked:
                    found = jnp.where(iota((CHUNK, STEP), 0) <= limit - at, found, NEG_FILL)
                scores[part * size + at : part * size + at + CHUNK, :] = found
                for row in range(0, CHUNK, WIDE):
                    tile = found[row : row + WIDE]
                    top = tile if top is None else jnp.maximum(top, tile)
        peaks[...] = jnp.max(top, axis=0, keepdims=True)

    def weigh(step, size, scores, peaks):
        peak = peaks[...]
        total = jnp.zeros((HEAD_DIM + ONES, STEP), jnp.float32)
        for part in range(2):
            weights = []
            for at in range(part * size, (part + 1) * size, CHUNK):
                weight = jnp.exp2((scores[at : at + CHUNK, :] - peak) * EXP2_SCALE)
                weights.append(weight.astype(jnp.bfloat16))
            total = total + jnp.dot(
                values[:, part * gathered : part * gathered + size],
                jnp.concatenate(weights, axis=0),
                preferred_element_type=jnp.float32,
            )
        mass = total[HEAD_DIM : HEAD_DIM + 1]
        outcome = (total[:HEAD_DIM] * (1.0 / mass)).astype(jnp.bfloat16)
        rest = jnp.where(peak > 0.5 * NEG_FILL, peak * SCORE_SCALE + jnp.log(mass), NEG_FILL)
        stat = jnp.zeros((STAT_ROWS, STEP), jnp.float32)
        row = iota((STAT_ROWS, STEP), 0)
        for piece in range(3):
            part = rest.astype(jnp.bfloat16).astype(jnp.float32)
            stat = jnp.where(row == piece, part, stat)
            rest = rest - part
        stat = stat.astype(jnp.bfloat16)
        for half in range(STEP // HEAD_DIM):
            tile = step * (STEP // HEAD_DIM) + half
            y = tile // (ROWS // HEAD_DIM)
            lanes = pl.ds(
                pl.multiple_of(lax.rem(tile, ROWS // HEAD_DIM) * HEAD_DIM, HEAD_DIM), HEAD_DIM
            )
            columns = slice(half * HEAD_DIM, (half + 1) * HEAD_DIM)
            out_ref[y, :HEAD_DIM, lanes] = outcome[:, columns]
            out_ref[y, HEAD_DIM:, lanes] = stat[:, columns]

    def all_steps(size, masked):
        even, odd = (scores_even, peaks_even), (scores_odd, peaks_odd)
        steps = Y * ROWS // STEP
        score(0, size, masked, *even)
        for part, (source, _) in enumerate(sources):
            values[:HEAD_DIM, part * gathered : part * gathered + size] = source[:size, HEAD_DIM:].T
        values[HEAD_DIM:, :] = jnp.ones((ONES, CORES * gathered), jnp.bfloat16)

        def two(pair, carry):
            step = 2 * pair
            score(step + 1, size, masked, *odd)
            weigh(step, size, *even)
            score(step + 2, size, masked, *even)
            weigh(step + 1, size, *odd)
            return carry

        lax.fori_loop(0, steps // 2 - 1, two, 0)
        score(steps - 1, size, masked, *odd)
        weigh(steps - 2, size, *even)
        weigh(steps - 1, size, *odd)

    @pl.when(z_own == Z_HI - 1)
    def _():
        all_steps(gathered, gathered - GROUP_LEN)

    @pl.when(z_own != Z_HI - 1)
    def _():
        all_steps(SHORT, 0)


def merge_kernel(count_ref, parts_ref, out_ref):
    live = iota((SLOTS, HEAD_DIM), 0) < count_ref[0]
    levels = []
    for y in range(Y):
        stat = parts_ref[y, HEAD_DIM:, :].astype(jnp.float32)
        levels.append(stat[0:1] + stat[1:2] + stat[2:3])
    top = functools.reduce(jnp.maximum, levels)
    shares = [jnp.exp(level - top) for level in levels]
    scale = 1.0 / functools.reduce(jnp.add, shares)
    for k in range(ROWS // HEAD_DIM):
        lanes = slice(k * HEAD_DIM, (k + 1) * HEAD_DIM)
        total = jnp.zeros((HEAD_DIM, HEAD_DIM), jnp.float32)
        for y in range(Y):
            part = parts_ref[y, :HEAD_DIM, lanes].astype(jnp.float32)
            total = total + (shares[y] * scale)[:, lanes] * part
        rows = total.T
        for at in range(0, HEAD_DIM, 16):
            head, slot = divmod(k * HEAD_DIM + at, SLOTS)
            found = jnp.where(live[slot : slot + 16], rows[at : at + 16], 0.0)
            out_ref[slot : slot + 16, head * HEAD_DIM : (head + 1) * HEAD_DIM] = found.astype(
                jnp.bfloat16
            )


def kernel_params(mib):
    return pltpu.CompilerParams(vmem_limit_bytes=mib << 20)


def shards(
    queries,
    cached_keys,
    cached_values,
    fresh_keys,
    fresh_values,
    recompute_index,
    recompute_count,
    group_offsets,
):
    bf16, f32 = jnp.bfloat16, jnp.float32
    shape = jax.ShapeDtypeStruct
    freq = inverse_freq()
    freq = jnp.concatenate([freq, freq])[None, :]
    copies, own_kv, joined_keys, joined_values, squares = pl.pallas_call(
        prepare_kernel,
        out_shape=(
            shape((Y, ROWS, HEAD_DIM), bf16),
            shape((GROUP_LEN, 2 * HEAD_DIM), bf16),
            shape((GROUP_LEN, HEAD_DIM), bf16),
            shape((GROUP_LEN, HEAD_DIM), bf16),
            shape((1, SLOTS), f32),
        ),
        in_specs=[SMEM, SMEM, VMEM] + [HBM] * 6,
        out_specs=[HBM] + [VMEM] * 4,
        scratch_shapes=[
            pltpu.VMEM((1, SLOTS), jnp.int32),
            pltpu.VMEM((SLOTS, HEADS_PER * HEAD_DIM), bf16),
            pltpu.VMEM((GROUP_LEN, HEAD_DIM), bf16),
            pltpu.VMEM((GROUP_LEN, HEAD_DIM), bf16),
            pltpu.VMEM((SLOTS, HEAD_DIM), bf16),
            pltpu.VMEM((SLOTS, HEAD_DIM), bf16),
            pltpu.VMEM((ROWS, HEAD_DIM), bf16),
            pltpu.SemaphoreType.DMA((6,)),
            pltpu.SemaphoreType.DMA((Y,)),
        ],
        name="prepare",
    )(
        group_offsets, recompute_count, freq, recompute_index,
        queries, cached_keys, cached_values, fresh_keys, fresh_values,
    )

    all_queries = lax.all_to_all(
        copies, "ctx", 0, 0, axis_index_groups=QUERY_GROUPS, tiled=True
    )
    core_kv = lax.all_gather(own_kv, "ctx", axis=0, axis_index_groups=KEY_GROUPS, tiled=True)
    other_kv = lax.ppermute(core_kv, "ctx", CORE_SWAP)

    score_shape = pltpu.VMEM((CORES * Z_HI * GROUP_LEN, STEP), f32)
    partial = pl.pallas_call(
        attend_kernel,
        out_shape=shape((Y, HEAD_DIM + STAT_ROWS, ROWS), bf16),
        in_specs=[VMEM] * 4,
        out_specs=VMEM,
        scratch_shapes=[
            pltpu.VMEM((HEAD_DIM + ONES, CORES * Z_HI * GROUP_LEN), bf16),
            pltpu.VMEM((1, Y * ROWS), jnp.int32),
            pltpu.VMEM((1, Y * ROWS), jnp.int32),
            score_shape,
            score_shape,
            pltpu.VMEM((1, STEP), f32),
            pltpu.VMEM((1, STEP), f32),
        ],
        compiler_params=kernel_params(28),
        name="attend",
    )(recompute_index, all_queries.reshape(Y * ROWS, HEAD_DIM), core_kv, other_kv)

    parts = lax.all_to_all(
        partial, "ctx", 0, 0, axis_index_groups=QUERY_GROUPS, tiled=True
    )
    squares = lax.all_gather(squares, "head", axis=0, tiled=True)
    drift = squares.sum(axis=0, keepdims=True)
    drift = drift / (2.0 * KV_HEADS * HEAD_DIM)
    drift = jnp.where(iota((1, SLOTS), 1) < recompute_count[0], drift, 0.0)

    attention = pl.pallas_call(
        merge_kernel,
        out_shape=shape((SLOTS, HEADS_PER * HEAD_DIM), bf16),
        in_specs=[SMEM, VMEM],
        out_specs=VMEM,
        compiler_params=kernel_params(16),
        name="merge",
    )(recompute_count, parts)
    return (attention, joined_keys, joined_values, drift)


def solution(mesh):
    return jax.shard_map(
        shards,
        mesh=mesh,
        in_specs=(
            P("ctx", "head"),
            P("ctx", "head"),
            P("ctx", "head"),
            P("ctx", "head"),
            P("ctx", "head"),
            P("ctx", None),
            P("ctx"),
            P(),
        ),
        out_specs=(P("ctx", "head"), P("ctx", "head"), P("ctx", "head"), P("ctx", None)),
        check_vma=False,
    )
```

```python
import functools
import math

import jax
import jax.numpy as jnp
from jax import lax
from jax.experimental import pallas as pl
from jax.experimental.pallas import tpu as pltpu
from jax.sharding import PartitionSpec as P


HEADS = 64
KV_HEADS = 8
HEAD_DIM = 128
HEADS_PER = HEADS // KV_HEADS
Z_HI, Y, CORES = 4, 8, 2
SLOTS = 48
GROUP_LEN = 320
ROWS = SLOTS * HEADS_PER
STAT_ROWS = 8
ONES = 16
STEP = 256
CHUNK = 256
WIDE = 64
SHORT = 1024
NEG_FILL = -1e30
EXP2_SCALE = math.log2(math.e) / math.sqrt(HEAD_DIM)
SCORE_SCALE = 1.0 / math.sqrt(HEAD_DIM)

VMEM = pl.BlockSpec(memory_space=pltpu.VMEM)
SMEM = pl.BlockSpec(memory_space=pltpu.SMEM)
HBM = pl.BlockSpec(memory_space=pltpu.HBM)


def ctx_index(z_hi, y, core):
    return (z_hi * Y + y) * CORES + core


QUERY_ORDERS = [list(range(Y)), list(range(Y - 1, -1, -1))]
QUERY_GROUPS = [
    [ctx_index(z, y, c) for y in QUERY_ORDERS[c]] for z in range(Z_HI) for c in range(CORES)
]
KEY_GROUPS = [[ctx_index(z, y, c) for z in range(Z_HI)] for y in range(Y) for c in range(CORES)]
CORE_SWAP = [(i, i ^ 1) for i in range(Z_HI * Y * CORES)]


def inverse_freq():
    half_dim = HEAD_DIM // 2
    exponent = jnp.arange(half_dim, dtype=jnp.float32) * 2.0 / HEAD_DIM
    base_freq = 1.0 / 500000.0**exponent
    wavelength = 2.0 * jnp.pi / base_freq
    smooth = (8192.0 / wavelength - 1.0) / 3.0
    blended_freq = (1.0 - smooth) * base_freq / 8.0 + smooth * base_freq
    return jnp.where(
        wavelength < 2048.0,
        base_freq,
        jnp.where(wavelength > 8192.0, base_freq / 8.0, blended_freq),
    )


def iota(shape, dim):
    return lax.broadcasted_iota(jnp.int32, shape, dim)


def column_of(row):
    n = row.shape[1]
    eye = iota((n, n), 0) == iota((n, n), 1)
    return jnp.sum(jnp.where(eye, jnp.broadcast_to(row, (n, n)), 0.0), axis=1, keepdims=True)


def row_of(wide):
    n = wide.shape[0]
    eye = iota((n, n), 0) == iota((n, n), 1)
    return jnp.sum(jnp.where(eye, wide, 0.0), axis=0, keepdims=True)


def prepare_kernel(
    offsets, count_ref, freq_ref, index_hbm, q_hbm, ck_hbm, cv_hbm, fk_hbm, fv_hbm,
    q_out, kv_out, jk_out, jv_out, drift_out,
    index_ref, q_ref, ck_ref, cv_ref, fk_ref, fv_ref, arrived,
):
    copies = [
        pltpu.make_async_copy(source, target, arrived.at[i])
        for i, (source, target) in enumerate((
            (index_hbm, index_ref), (q_hbm, q_ref), (fk_hbm, fk_ref),
            (ck_hbm, ck_ref), (fv_hbm, fv_ref), (cv_hbm, cv_ref),
        ))
    ]
    for copy in copies:
        copy.start()
    copies[0].wait()
    own_start = offsets[lax.axis_index("ctx")]
    count = count_ref[0]
    half = HEAD_DIM // 2
    index_row = index_ref[...]
    index_col = column_of(index_row.astype(jnp.float32))
    freq = freq_ref[...]
    start_row = jnp.full((1, HEAD_DIM), own_start, jnp.int32).astype(jnp.float32)
    slot_angle = (index_col + start_row[:, :1]) * freq
    group_angle = start_row * freq
    sign = jnp.where(iota((1, HEAD_DIM), 1) < half, -1.0, 1.0)
    slot_cos, slot_sin = jnp.cos(slot_angle), jnp.sin(slot_angle) * sign
    group_cos, group_sin = jnp.cos(group_angle), jnp.sin(group_angle) * sign

    def turn(rows, cosine, sine):
        x = rows.astype(jnp.float32)
        return (x * cosine + pltpu.roll(x, half, 1) * sine).astype(jnp.bfloat16)

    copies[1].wait()
    for h in range(HEADS_PER):
        head = turn(q_ref[:, h * HEAD_DIM : (h + 1) * HEAD_DIM], slot_cos, slot_sin)
        for y in range(Y):
            q_out[y, h * SLOTS : (h + 1) * SLOTS, :] = head

    for copy in copies[2:]:
        copy.wait()
    turned = turn(ck_ref[...], group_cos, group_sin)
    fresh = turn(fk_ref[...], slot_cos, slot_sin)
    cached_values = cv_ref[...]
    fresh_values = fv_ref[...]

    live = iota((1, SLOTS), 1) < count
    chosen = jnp.where(live, index_row, -1)
    picker = jnp.where(iota((GROUP_LEN, SLOTS), 0) == chosen, 1.0, 0.0)
    covered = jnp.sum(picker, axis=1, keepdims=True) > 0.0
    picker = picker.astype(jnp.bfloat16)
    joined_keys = jnp.where(
        covered,
        jnp.dot(picker, fresh, preferred_element_type=jnp.float32),
        turned.astype(jnp.float32),
    ).astype(jnp.bfloat16)
    joined_values = jnp.where(
        covered,
        jnp.dot(picker, fresh_values, preferred_element_type=jnp.float32),
        cached_values.astype(jnp.float32),
    ).astype(jnp.bfloat16)
    jk_out[...] = joined_keys
    jv_out[...] = joined_values
    kv_out[:, :HEAD_DIM] = joined_keys
    kv_out[:, HEAD_DIM:] = joined_values

    reader = jnp.where(
        iota((SLOTS, GROUP_LEN), 1).astype(jnp.float32) == index_col, 1.0, 0.0
    ).astype(jnp.bfloat16)
    key_gap = fresh.astype(jnp.float32) - jnp.dot(
        reader, turned, preferred_element_type=jnp.float32
    )
    value_gap = fresh_values.astype(jnp.float32) - jnp.dot(
        reader, cached_values, preferred_element_type=jnp.float32
    )
    squares = jnp.sum(key_gap * key_gap + value_gap * value_gap, axis=1, keepdims=True)
    drift_row = row_of(jnp.broadcast_to(squares, (SLOTS, SLOTS)))
    drift_out[...] = drift_row


def attend_kernel(
    index_ref, q_ref, own_ref, other_ref, out_ref, values, own_limit, other_limit,
    scores_even, scores_odd, peaks_even, peaks_odd,
):
    me = lax.axis_index("ctx")
    core = lax.rem(me, CORES)
    y_own = lax.rem(me // CORES, Y)
    z_own = me // (CORES * Y)
    gathered = Z_HI * GROUP_LEN
    sources = (own_ref, own_limit), (other_ref, other_limit)

    index_col = column_of(index_ref[...].astype(jnp.float32))
    slot = lax.rem(iota((SLOTS, ROWS), 1), SLOTS)
    own_index = jnp.sum(
        jnp.where(slot == iota((SLOTS, ROWS), 0), index_col, 0.0), axis=0, keepdims=True
    )
    before = z_own * GROUP_LEN - 1
    full = before + GROUP_LEN
    for place in range(Y):
        y = jnp.where(core == 1, QUERY_ORDERS[1][place], QUERY_ORDERS[0][place])
        lanes = slice(place * ROWS, (place + 1) * ROWS)
        beside = jnp.where(y_own < y, full, before)
        own_limit[:, lanes] = jnp.where(
            y == y_own, own_index.astype(jnp.int32) + (before + 1), beside
        )
        other_limit[:, lanes] = jnp.full(
            (1, ROWS), jnp.where(jnp.logical_and(y == y_own, core == 1), full, beside), jnp.int32
        )

    def score(step, size, masked, scores, peaks):
        lanes = pl.ds(pl.multiple_of(step * STEP, STEP), STEP)
        queries = q_ref[lanes, :]
        top = None
        for part, (source, limit_ref) in enumerate(sources):
            limit = limit_ref[:, lanes]
            for at in range(0, size, CHUNK):
                found = lax.dot_general(
                    source[at : at + CHUNK, :HEAD_DIM],
                    queries,
                    (((1,), (1,)), ((), ())),
                    preferred_element_type=jnp.float32,
                )
                if at + CHUNK > masked:
                    found = jnp.where(iota((CHUNK, STEP), 0) <= limit - at, found, NEG_FILL)
                scores[part * size + at : part * size + at + CHUNK, :] = found
                for row in range(0, CHUNK, WIDE):
                    tile = found[row : row + WIDE]
                    top = tile if top is None else jnp.maximum(top, tile)
        peaks[...] = jnp.max(top, axis=0, keepdims=True)

    def weigh(step, size, scores, peaks):
        peak = peaks[...]
        total = jnp.zeros((HEAD_DIM + ONES, STEP), jnp.float32)
        for part in range(2):
            weights = []
            for at in range(part * size, (part + 1) * size, CHUNK):
                weight = jnp.exp2((scores[at : at + CHUNK, :] - peak) * EXP2_SCALE)
                weights.append(weight.astype(jnp.bfloat16))
            total = total + jnp.dot(
                values[:, part * gathered : part * gathered + size],
                jnp.concatenate(weights, axis=0),
                preferred_element_type=jnp.float32,
            )
        mass = total[HEAD_DIM : HEAD_DIM + 1]
        outcome = (total[:HEAD_DIM] * (1.0 / mass)).astype(jnp.bfloat16)
        rest = jnp.where(peak > 0.5 * NEG_FILL, peak * SCORE_SCALE + jnp.log(mass), NEG_FILL)
        stat = jnp.zeros((STAT_ROWS, STEP), jnp.float32)
        row = iota((STAT_ROWS, STEP), 0)
        for piece in range(3):
            part = rest.astype(jnp.bfloat16).astype(jnp.float32)
            stat = jnp.where(row == piece, part, stat)
            rest = rest - part
        stat = stat.astype(jnp.bfloat16)
        for half in range(STEP // HEAD_DIM):
            tile = step * (STEP // HEAD_DIM) + half
            place = tile // (ROWS // HEAD_DIM)
            lanes = pl.ds(
                pl.multiple_of(lax.rem(tile, ROWS // HEAD_DIM) * HEAD_DIM, HEAD_DIM), HEAD_DIM
            )
            columns = slice(half * HEAD_DIM, (half + 1) * HEAD_DIM)
            out_ref[place, :HEAD_DIM, lanes] = outcome[:, columns]
            out_ref[place, HEAD_DIM:, lanes] = stat[:, columns]

    def all_steps(size, masked):
        even, odd = (scores_even, peaks_even), (scores_odd, peaks_odd)
        steps = Y * ROWS // STEP
        score(0, size, masked, *even)
        for part, (source, _) in enumerate(sources):
            values[:HEAD_DIM, part * gathered : part * gathered + size] = source[:size, HEAD_DIM:].T
        values[HEAD_DIM:, :] = jnp.ones((ONES, CORES * gathered), jnp.bfloat16)

        def two(pair, carry):
            step = 2 * pair
            score(step + 1, size, masked, *odd)
            weigh(step, size, *even)
            score(step + 2, size, masked, *even)
            weigh(step + 1, size, *odd)
            return carry

        lax.fori_loop(0, steps // 2 - 1, two, 0)
        score(steps - 1, size, masked, *odd)
        weigh(steps - 2, size, *even)
        weigh(steps - 1, size, *odd)

    @pl.when(z_own == Z_HI - 1)
    def _():
        all_steps(gathered, gathered - GROUP_LEN)

    @pl.when(z_own != Z_HI - 1)
    def _():
        all_steps(SHORT, 0)


def merge_kernel(count_ref, parts_ref, out_ref):
    live = iota((SLOTS, HEAD_DIM), 0) < count_ref[0]
    levels = []
    for y in range(Y):
        stat = parts_ref[y, HEAD_DIM:, :].astype(jnp.float32)
        levels.append(stat[0:1] + stat[1:2] + stat[2:3])
    top = functools.reduce(jnp.maximum, levels)
    shares = [jnp.exp(level - top) for level in levels]
    scale = 1.0 / functools.reduce(jnp.add, shares)
    for k in range(ROWS // HEAD_DIM):
        lanes = slice(k * HEAD_DIM, (k + 1) * HEAD_DIM)
        total = jnp.zeros((HEAD_DIM, HEAD_DIM), jnp.float32)
        for y in range(Y):
            part = parts_ref[y, :HEAD_DIM, lanes].astype(jnp.float32)
            total = total + (shares[y] * scale)[:, lanes] * part
        rows = total.T
        for at in range(0, HEAD_DIM, 16):
            head, slot = divmod(k * HEAD_DIM + at, SLOTS)
            found = jnp.where(live[slot : slot + 16], rows[at : at + 16], 0.0)
            out_ref[slot : slot + 16, head * HEAD_DIM : (head + 1) * HEAD_DIM] = found.astype(
                jnp.bfloat16
            )


def kernel_params(mib):
    return pltpu.CompilerParams(vmem_limit_bytes=mib << 20)


def shards(
    queries,
    cached_keys,
    cached_values,
    fresh_keys,
    fresh_values,
    recompute_index,
    recompute_count,
    group_offsets,
):
    bf16, f32 = jnp.bfloat16, jnp.float32
    shape = jax.ShapeDtypeStruct
    freq = inverse_freq()
    freq = jnp.concatenate([freq, freq])[None, :]
    copies, own_kv, joined_keys, joined_values, squares = pl.pallas_call(
        prepare_kernel,
        out_shape=(
            shape((Y, ROWS, HEAD_DIM), bf16),
            shape((GROUP_LEN, 2 * HEAD_DIM), bf16),
            shape((GROUP_LEN, HEAD_DIM), bf16),
            shape((GROUP_LEN, HEAD_DIM), bf16),
            shape((1, SLOTS), f32),
        ),
        in_specs=[SMEM, SMEM, VMEM] + [HBM] * 6,
        out_specs=[VMEM] * 5,
        scratch_shapes=[
            pltpu.VMEM((1, SLOTS), jnp.int32),
            pltpu.VMEM((SLOTS, HEADS_PER * HEAD_DIM), bf16),
            pltpu.VMEM((GROUP_LEN, HEAD_DIM), bf16),
            pltpu.VMEM((GROUP_LEN, HEAD_DIM), bf16),
            pltpu.VMEM((SLOTS, HEAD_DIM), bf16),
            pltpu.VMEM((SLOTS, HEAD_DIM), bf16),
            pltpu.SemaphoreType.DMA((6,)),
        ],
        name="prepare",
    )(
        group_offsets, recompute_count, freq, recompute_index,
        queries, cached_keys, cached_values, fresh_keys, fresh_values,
    )

    all_queries = lax.all_to_all(
        copies, "ctx", 0, 0, axis_index_groups=QUERY_GROUPS, tiled=True
    )
    core_kv = lax.all_gather(own_kv, "ctx", axis=0, axis_index_groups=KEY_GROUPS, tiled=True)
    other_kv = lax.ppermute(core_kv, "ctx", CORE_SWAP)

    score_shape = pltpu.VMEM((CORES * Z_HI * GROUP_LEN, STEP), f32)
    partial = pl.pallas_call(
        attend_kernel,
        out_shape=shape((Y, HEAD_DIM + STAT_ROWS, ROWS), bf16),
        in_specs=[VMEM] * 4,
        out_specs=VMEM,
        scratch_shapes=[
            pltpu.VMEM((HEAD_DIM + ONES, CORES * Z_HI * GROUP_LEN), bf16),
            pltpu.VMEM((1, Y * ROWS), jnp.int32),
            pltpu.VMEM((1, Y * ROWS), jnp.int32),
            score_shape,
            score_shape,
            pltpu.VMEM((1, STEP), f32),
            pltpu.VMEM((1, STEP), f32),
        ],
        compiler_params=kernel_params(28),
        name="attend",
    )(recompute_index, all_queries.reshape(Y * ROWS, HEAD_DIM), core_kv, other_kv)

    parts = lax.all_to_all(
        partial, "ctx", 0, 0, axis_index_groups=QUERY_GROUPS, tiled=True
    )
    squares = lax.all_gather(squares, "head", axis=0, tiled=True)
    drift = squares.sum(axis=0, keepdims=True)
    drift = drift / (2.0 * KV_HEADS * HEAD_DIM)
    drift = jnp.where(iota((1, SLOTS), 1) < recompute_count[0], drift, 0.0)

    attention = pl.pallas_call(
        merge_kernel,
        out_shape=shape((SLOTS, HEADS_PER * HEAD_DIM), bf16),
        in_specs=[SMEM, VMEM],
        out_specs=VMEM,
        compiler_params=kernel_params(16),
        name="merge",
    )(recompute_count, parts)
    return (attention, joined_keys, joined_values, drift)


def solution(mesh):
    return jax.shard_map(
        shards,
        mesh=mesh,
        in_specs=(
            P("ctx", "head"),
            P("ctx", "head"),
            P("ctx", "head"),
            P("ctx", "head"),
            P("ctx", "head"),
            P("ctx", None),
            P("ctx"),
            P(),
        ),
        out_specs=(P("ctx", "head"), P("ctx", "head"), P("ctx", "head"), P("ctx", None)),
        check_vma=False,
    )
```

```python
import functools
import math

import jax
import jax.numpy as jnp
import numpy as np
from jax import lax
from jax.experimental import pallas as pl
from jax.experimental.pallas import tpu as pltpu
from jax.sharding import PartitionSpec as P


HEADS = 64
KV_HEADS = 8
HEAD_DIM = 128
HEADS_PER = HEADS // KV_HEADS
Z_HI, Y, CORES = 4, 8, 2
SLOTS = 48
GROUP_LEN = 320
ROWS = SLOTS * HEADS_PER
STAT_ROWS = 8
ONES = 16
STEP = 256
CHUNK = 256
WIDE = 64
SHORT = 1024
NEG_FILL = -1e30
EXP2_SCALE = math.log2(math.e) / math.sqrt(HEAD_DIM)
SCORE_SCALE = 1.0 / math.sqrt(HEAD_DIM)

VMEM = pl.BlockSpec(memory_space=pltpu.VMEM)
SMEM = pl.BlockSpec(memory_space=pltpu.SMEM)
HBM = pl.BlockSpec(memory_space=pltpu.HBM)


def ctx_index(z_hi, y, core):
    return (z_hi * Y + y) * CORES + core


QUERY_ORDERS = [list(range(Y)), list(range(Y - 1, -1, -1))]
QUERY_GROUPS = [
    [ctx_index(z, y, c) for y in QUERY_ORDERS[c]] for z in range(Z_HI) for c in range(CORES)
]
KEY_GROUPS = [[ctx_index(z, y, c) for z in range(Z_HI)] for y in range(Y) for c in range(CORES)]
CORE_SWAP = [(i, i ^ 1) for i in range(Z_HI * Y * CORES)]


def inverse_freq():
    base = 1.0 / 500000.0 ** (np.arange(HEAD_DIM // 2) * 2.0 / HEAD_DIM)
    wavelength = 2.0 * np.pi / base
    smooth = (8192.0 / wavelength - 1.0) / 3.0
    blended = (1.0 - smooth) * base / 8.0 + smooth * base
    freq = np.where(wavelength < 2048.0, base, np.where(wavelength > 8192.0, base / 8.0, blended))
    return [float(value) for value in freq.astype(np.float32)]


def iota(shape, dim):
    return lax.broadcasted_iota(jnp.int32, shape, dim)


def column_of(row):
    n = row.shape[1]
    eye = iota((n, n), 0) == iota((n, n), 1)
    return jnp.sum(jnp.where(eye, jnp.broadcast_to(row, (n, n)), 0.0), axis=1, keepdims=True)


def row_of(wide):
    n = wide.shape[0]
    eye = iota((n, n), 0) == iota((n, n), 1)
    return jnp.sum(jnp.where(eye, wide, 0.0), axis=0, keepdims=True)


def prepare_kernel(
    offsets, count_ref, index_hbm, q_hbm, ck_hbm, cv_hbm, fk_hbm, fv_hbm,
    q_out, kv_out, jk_out, jv_out, drift_out,
    index_ref, q_ref, ck_ref, cv_ref, fk_ref, fv_ref, copies_ref, kv_ref, drift_ref, arrived, left,
):
    copies = [
        pltpu.make_async_copy(source, target, arrived.at[i])
        for i, (source, target) in enumerate((
            (index_hbm, index_ref), (q_hbm, q_ref), (fk_hbm, fk_ref),
            (ck_hbm, ck_ref), (fv_hbm, fv_ref), (cv_hbm, cv_ref),
        ))
    ]
    for copy in copies:
        copy.start()
    sends = [
        pltpu.make_async_copy(source, target, left.at[i])
        for i, (source, target) in enumerate((
            (copies_ref, q_out),
            (kv_ref, kv_out),
            (kv_ref.at[:, :HEAD_DIM], jk_out),
            (kv_ref.at[:, HEAD_DIM:], jv_out),
            (drift_ref, drift_out),
        ))
    ]
    half = HEAD_DIM // 2
    lane = lax.rem(iota((1, HEAD_DIM), 1), half)
    freq = jnp.zeros((1, HEAD_DIM), jnp.float32)
    for i, value in enumerate(inverse_freq()):
        freq = jnp.where(lane == i, value, freq)
    own_start = offsets[lax.axis_index("ctx")]
    count = count_ref[0]
    copies[0].wait()
    index_row = index_ref[...]
    index_col = column_of(index_row.astype(jnp.float32))
    start_row = jnp.full((1, HEAD_DIM), own_start, jnp.int32).astype(jnp.float32)
    slot_angle = (index_col + start_row[:, :1]) * freq
    group_angle = start_row * freq
    sign = jnp.where(iota((1, HEAD_DIM), 1) < half, -1.0, 1.0)
    slot_cos, slot_sin = jnp.cos(slot_angle), jnp.sin(slot_angle) * sign
    group_cos, group_sin = jnp.cos(group_angle), jnp.sin(group_angle) * sign

    def turn(rows, cosine, sine):
        x = rows.astype(jnp.float32)
        return (x * cosine + pltpu.roll(x, half, 1) * sine).astype(jnp.bfloat16)

    copies[1].wait()
    for h in range(HEADS_PER):
        head = turn(q_ref[:, h * HEAD_DIM : (h + 1) * HEAD_DIM], slot_cos, slot_sin)
        for y in range(Y):
            copies_ref[y, h * SLOTS : (h + 1) * SLOTS, :] = head
    sends[0].start()

    for copy in copies[2:]:
        copy.wait()
    turned = turn(ck_ref[...], group_cos, group_sin)
    fresh = turn(fk_ref[...], slot_cos, slot_sin)
    cached_values = cv_ref[...]
    fresh_values = fv_ref[...]

    live = iota((1, SLOTS), 1) < count
    chosen = jnp.where(live, index_row, -1)
    picker = jnp.where(iota((GROUP_LEN, SLOTS), 0) == chosen, 1.0, 0.0)
    covered = jnp.sum(picker, axis=1, keepdims=True) > 0.0
    picker = picker.astype(jnp.bfloat16)
    joined_keys = jnp.where(
        covered,
        jnp.dot(picker, fresh, preferred_element_type=jnp.float32),
        turned.astype(jnp.float32),
    ).astype(jnp.bfloat16)
    joined_values = jnp.where(
        covered,
        jnp.dot(picker, fresh_values, preferred_element_type=jnp.float32),
        cached_values.astype(jnp.float32),
    ).astype(jnp.bfloat16)
    kv_ref[:, :HEAD_DIM] = joined_keys
    kv_ref[:, HEAD_DIM:] = joined_values
    for send in sends[1:4]:
        send.start()

    reader = jnp.where(
        iota((SLOTS, GROUP_LEN), 1).astype(jnp.float32) == index_col, 1.0, 0.0
    ).astype(jnp.bfloat16)
    key_gap = fresh.astype(jnp.float32) - jnp.dot(
        reader, turned, preferred_element_type=jnp.float32
    )
    value_gap = fresh_values.astype(jnp.float32) - jnp.dot(
        reader, cached_values, preferred_element_type=jnp.float32
    )
    squares = jnp.sum(key_gap * key_gap + value_gap * value_gap, axis=1, keepdims=True)
    drift_row = row_of(jnp.broadcast_to(squares, (SLOTS, SLOTS)))
    drift_ref[...] = drift_row
    sends[4].start()
    for send in sends:
        send.wait()


def attend_kernel(
    index_ref, q_ref, own_ref, other_ref, out_hbm, values, own_limit, other_limit,
    scores_even, scores_odd, peaks_even, peaks_odd, out_ref, left,
):
    me = lax.axis_index("ctx")
    core = lax.rem(me, CORES)
    y_own = lax.rem(me // CORES, Y)
    z_own = me // (CORES * Y)
    gathered = Z_HI * GROUP_LEN
    sources = (own_ref, own_limit), (other_ref, other_limit)

    index_col = column_of(index_ref[...].astype(jnp.float32))
    slot = lax.rem(iota((SLOTS, ROWS), 1), SLOTS)
    own_index = jnp.sum(
        jnp.where(slot == iota((SLOTS, ROWS), 0), index_col, 0.0), axis=0, keepdims=True
    )
    before = z_own * GROUP_LEN - 1
    full = before + GROUP_LEN
    for place in range(Y):
        y = jnp.where(core == 1, QUERY_ORDERS[1][place], QUERY_ORDERS[0][place])
        lanes = slice(place * ROWS, (place + 1) * ROWS)
        beside = jnp.where(y_own < y, full, before)
        own_limit[:, lanes] = jnp.where(
            y == y_own, own_index.astype(jnp.int32) + (before + 1), beside
        )
        other_limit[:, lanes] = jnp.full(
            (1, ROWS), jnp.where(jnp.logical_and(y == y_own, core == 1), full, beside), jnp.int32
        )

    def score(step, size, masked, scores, peaks):
        lanes = pl.ds(pl.multiple_of(step * STEP, STEP), STEP)
        queries = q_ref[lanes, :]
        top = None
        for part, (source, limit_ref) in enumerate(sources):
            limit = limit_ref[:, lanes]
            for at in range(0, size, CHUNK):
                found = lax.dot_general(
                    source[at : at + CHUNK, :HEAD_DIM],
                    queries,
                    (((1,), (1,)), ((), ())),
                    preferred_element_type=jnp.float32,
                )
                if at + CHUNK > masked:
                    found = jnp.where(iota((CHUNK, STEP), 0) <= limit - at, found, NEG_FILL)
                scores[part * size + at : part * size + at + CHUNK, :] = found
                for row in range(0, CHUNK, WIDE):
                    tile = found[row : row + WIDE]
                    top = tile if top is None else jnp.maximum(top, tile)
        peaks[...] = jnp.max(top, axis=0, keepdims=True)

    def weigh(step, size, scores, peaks):
        peak = peaks[...]
        total = jnp.zeros((HEAD_DIM + ONES, STEP), jnp.float32)
        for part in range(2):
            weights = []
            for at in range(part * size, (part + 1) * size, CHUNK):
                weight = jnp.exp2((scores[at : at + CHUNK, :] - peak) * EXP2_SCALE)
                weights.append(weight.astype(jnp.bfloat16))
            total = total + jnp.dot(
                values[:, part * gathered : part * gathered + size],
                jnp.concatenate(weights, axis=0),
                preferred_element_type=jnp.float32,
            )
        mass = total[HEAD_DIM : HEAD_DIM + 1]
        outcome = (total[:HEAD_DIM] * (1.0 / mass)).astype(jnp.bfloat16)
        rest = jnp.where(peak > 0.5 * NEG_FILL, peak * SCORE_SCALE + jnp.log(mass), NEG_FILL)
        stat = jnp.zeros((STAT_ROWS, STEP), jnp.float32)
        row = iota((STAT_ROWS, STEP), 0)
        for piece in range(3):
            part = rest.astype(jnp.bfloat16).astype(jnp.float32)
            stat = jnp.where(row == piece, part, stat)
            rest = rest - part
        stat = stat.astype(jnp.bfloat16)
        for half in range(STEP // HEAD_DIM):
            tile = step * (STEP // HEAD_DIM) + half
            place = tile // (ROWS // HEAD_DIM)
            lanes = pl.ds(
                pl.multiple_of(lax.rem(tile, ROWS // HEAD_DIM) * HEAD_DIM, HEAD_DIM), HEAD_DIM
            )
            columns = slice(half * HEAD_DIM, (half + 1) * HEAD_DIM)
            out_ref[place, :HEAD_DIM, lanes] = outcome[:, columns]
            out_ref[place, HEAD_DIM:, lanes] = stat[:, columns]

    def all_steps(size, masked):
        even, odd = (scores_even, peaks_even), (scores_odd, peaks_odd)
        steps = Y * ROWS // STEP
        score(0, size, masked, *even)
        for part, (source, _) in enumerate(sources):
            values[:HEAD_DIM, part * gathered : part * gathered + size] = source[:size, HEAD_DIM:].T
        values[HEAD_DIM:, :] = jnp.ones((ONES, CORES * gathered), jnp.bfloat16)

        def two(pair, carry):
            step = 2 * pair
            score(step + 1, size, masked, *odd)
            weigh(step, size, *even)
            score(step + 2, size, masked, *even)
            weigh(step + 1, size, *odd)
            return carry

        lax.fori_loop(0, steps // 2 - 1, two, 0)
        done = (steps - 2) * STEP // ROWS
        first = pltpu.make_async_copy(out_ref.at[:done], out_hbm.at[:done], left.at[0])
        first.start()
        score(steps - 1, size, masked, *odd)
        weigh(steps - 2, size, *even)
        weigh(steps - 1, size, *odd)
        last = pltpu.make_async_copy(out_ref.at[done:], out_hbm.at[done:], left.at[1])
        last.start()
        first.wait()
        last.wait()

    @pl.when(z_own == Z_HI - 1)
    def _():
        all_steps(gathered, gathered - GROUP_LEN)

    @pl.when(z_own != Z_HI - 1)
    def _():
        all_steps(SHORT, 0)


def merge_kernel(count_ref, parts_ref, out_ref):
    live = iota((SLOTS, HEAD_DIM), 0) < count_ref[0]
    levels = []
    for y in range(Y):
        stat = parts_ref[y, HEAD_DIM:, :].astype(jnp.float32)
        levels.append(stat[0:1] + stat[1:2] + stat[2:3])
    top = functools.reduce(jnp.maximum, levels)
    shares = [jnp.exp(level - top) for level in levels]
    scale = 1.0 / functools.reduce(jnp.add, shares)
    for k in range(ROWS // HEAD_DIM):
        lanes = slice(k * HEAD_DIM, (k + 1) * HEAD_DIM)
        total = jnp.zeros((HEAD_DIM, HEAD_DIM), jnp.float32)
        for y in range(Y):
            part = parts_ref[y, :HEAD_DIM, lanes].astype(jnp.float32)
            total = total + (shares[y] * scale)[:, lanes] * part
        rows = total.T
        for at in range(0, HEAD_DIM, 16):
            head, slot = divmod(k * HEAD_DIM + at, SLOTS)
            found = jnp.where(live[slot : slot + 16], rows[at : at + 16], 0.0)
            out_ref[slot : slot + 16, head * HEAD_DIM : (head + 1) * HEAD_DIM] = found.astype(
                jnp.bfloat16
            )


def kernel_params(mib):
    return pltpu.CompilerParams(vmem_limit_bytes=mib << 20)


def shards(
    queries,
    cached_keys,
    cached_values,
    fresh_keys,
    fresh_values,
    recompute_index,
    recompute_count,
    group_offsets,
):
    bf16, f32 = jnp.bfloat16, jnp.float32
    shape = jax.ShapeDtypeStruct
    copies, own_kv, joined_keys, joined_values, squares = pl.pallas_call(
        prepare_kernel,
        out_shape=(
            shape((Y, ROWS, HEAD_DIM), bf16),
            shape((GROUP_LEN, 2 * HEAD_DIM), bf16),
            shape((GROUP_LEN, HEAD_DIM), bf16),
            shape((GROUP_LEN, HEAD_DIM), bf16),
            shape((1, SLOTS), f32),
        ),
        in_specs=[SMEM, SMEM] + [HBM] * 6,
        out_specs=[HBM] * 5,
        scratch_shapes=[
            pltpu.VMEM((1, SLOTS), jnp.int32),
            pltpu.VMEM((SLOTS, HEADS_PER * HEAD_DIM), bf16),
            pltpu.VMEM((GROUP_LEN, HEAD_DIM), bf16),
            pltpu.VMEM((GROUP_LEN, HEAD_DIM), bf16),
            pltpu.VMEM((SLOTS, HEAD_DIM), bf16),
            pltpu.VMEM((SLOTS, HEAD_DIM), bf16),
            pltpu.VMEM((Y, ROWS, HEAD_DIM), bf16),
            pltpu.VMEM((GROUP_LEN, 2 * HEAD_DIM), bf16),
            pltpu.VMEM((1, SLOTS), f32),
            pltpu.SemaphoreType.DMA((6,)),
            pltpu.SemaphoreType.DMA((5,)),
        ],
        name="prepare",
    )(
        group_offsets, recompute_count, recompute_index,
        queries, cached_keys, cached_values, fresh_keys, fresh_values,
    )

    all_queries = lax.all_to_all(
        copies, "ctx", 0, 0, axis_index_groups=QUERY_GROUPS, tiled=True
    )
    core_kv = lax.all_gather(own_kv, "ctx", axis=0, axis_index_groups=KEY_GROUPS, tiled=True)
    other_kv = lax.ppermute(core_kv, "ctx", CORE_SWAP)

    score_shape = pltpu.VMEM((CORES * Z_HI * GROUP_LEN, STEP), f32)
    partial = pl.pallas_call(
        attend_kernel,
        out_shape=shape((Y, HEAD_DIM + STAT_ROWS, ROWS), bf16),
        in_specs=[VMEM] * 4,
        out_specs=HBM,
        scratch_shapes=[
            pltpu.VMEM((HEAD_DIM + ONES, CORES * Z_HI * GROUP_LEN), bf16),
            pltpu.VMEM((1, Y * ROWS), jnp.int32),
            pltpu.VMEM((1, Y * ROWS), jnp.int32),
            score_shape,
            score_shape,
            pltpu.VMEM((1, STEP), f32),
            pltpu.VMEM((1, STEP), f32),
            pltpu.VMEM((Y, HEAD_DIM + STAT_ROWS, ROWS), bf16),
            pltpu.SemaphoreType.DMA((2,)),
        ],
        compiler_params=kernel_params(28),
        name="attend",
    )(recompute_index, all_queries.reshape(Y * ROWS, HEAD_DIM), core_kv, other_kv)

    parts = lax.all_to_all(
        partial, "ctx", 0, 0, axis_index_groups=QUERY_GROUPS, tiled=True
    )
    squares = lax.all_gather(squares, "head", axis=0, tiled=True)
    drift = squares.sum(axis=0, keepdims=True)
    drift = drift / (2.0 * KV_HEADS * HEAD_DIM)
    drift = jnp.where(iota((1, SLOTS), 1) < recompute_count[0], drift, 0.0)

    attention = pl.pallas_call(
        merge_kernel,
        out_shape=shape((SLOTS, HEADS_PER * HEAD_DIM), bf16),
        in_specs=[SMEM, VMEM],
        out_specs=VMEM,
        compiler_params=kernel_params(16),
        name="merge",
    )(recompute_count, parts)
    return (attention, joined_keys, joined_values, drift)


def solution(mesh):
    return jax.shard_map(
        shards,
        mesh=mesh,
        in_specs=(
            P("ctx", "head"),
            P("ctx", "head"),
            P("ctx", "head"),
            P("ctx", "head"),
            P("ctx", "head"),
            P("ctx", None),
            P("ctx"),
            P(),
        ),
        out_specs=(P("ctx", "head"), P("ctx", "head"), P("ctx", "head"), P("ctx", None)),
        check_vma=False,
    )
```

```python
import functools
import math

import jax
import jax.numpy as jnp
import numpy as np
from jax import lax
from jax.experimental import pallas as pl
from jax.experimental.pallas import tpu as pltpu
from jax.sharding import PartitionSpec as P


HEADS = 64
KV_HEADS = 8
HEAD_DIM = 128
HEADS_PER = HEADS // KV_HEADS
Z_HI, Y, CORES = 4, 8, 2
SLOTS = 48
GROUP_LEN = 320
ROWS = SLOTS * HEADS_PER
STAT_ROWS = 8
ONES = 16
STEP = 256
CHUNK = 256
WIDE = 64
SHORT = 1024
NEG_FILL = -1e30
EXP2_SCALE = math.log2(math.e) / math.sqrt(HEAD_DIM)
SCORE_SCALE = 1.0 / math.sqrt(HEAD_DIM)

VMEM = pl.BlockSpec(memory_space=pltpu.VMEM)
HBM = pl.BlockSpec(memory_space=pltpu.HBM)


def ctx_index(z_hi, y, core):
    return (z_hi * Y + y) * CORES + core


QUERY_ORDERS = [list(range(Y)), list(range(Y - 1, -1, -1))]
QUERY_GROUPS = [
    [ctx_index(z, y, c) for y in QUERY_ORDERS[c]] for z in range(Z_HI) for c in range(CORES)
]
KEY_GROUPS = [[ctx_index(z, y, c) for z in range(Z_HI)] for y in range(Y) for c in range(CORES)]
CORE_SWAP = [(i, i ^ 1) for i in range(Z_HI * Y * CORES)]


def inverse_freq():
    base = 1.0 / 500000.0 ** (np.arange(HEAD_DIM // 2) * 2.0 / HEAD_DIM)
    wavelength = 2.0 * np.pi / base
    smooth = (8192.0 / wavelength - 1.0) / 3.0
    blended = (1.0 - smooth) * base / 8.0 + smooth * base
    freq = np.where(wavelength < 2048.0, base, np.where(wavelength > 8192.0, base / 8.0, blended))
    return [float(value) for value in freq.astype(np.float32)]


def iota(shape, dim):
    return lax.broadcasted_iota(jnp.int32, shape, dim)


def column_of(row):
    n = row.shape[1]
    eye = iota((n, n), 0) == iota((n, n), 1)
    return jnp.sum(jnp.where(eye, jnp.broadcast_to(row, (n, n)), 0.0), axis=1, keepdims=True)


def row_of(wide):
    n = wide.shape[0]
    eye = iota((n, n), 0) == iota((n, n), 1)
    return jnp.sum(jnp.where(eye, wide, 0.0), axis=0, keepdims=True)


def prepare_kernel(
    offsets_hbm, count_hbm, index_hbm, q_hbm, ck_hbm, cv_hbm, fk_hbm, fv_hbm,
    q_out, kv_out, jk_out, jv_out, drift_out,
    offsets_ref, count_ref, index_ref, q_ref, ck_ref, cv_ref, fk_ref, fv_ref, copies_ref, kv_ref, drift_ref,
    arrived, left,
):
    copies = [
        pltpu.make_async_copy(source, target, arrived.at[i])
        for i, (source, target) in enumerate((
            (offsets_hbm, offsets_ref), (count_hbm, count_ref), (index_hbm, index_ref),
            (q_hbm, q_ref), (fk_hbm, fk_ref), (ck_hbm, ck_ref), (fv_hbm, fv_ref), (cv_hbm, cv_ref),
        ))
    ]
    for copy in copies:
        copy.start()
    sends = [
        pltpu.make_async_copy(source, target, left.at[i])
        for i, (source, target) in enumerate((
            (copies_ref, q_out),
            (kv_ref, kv_out),
            (kv_ref.at[:, :HEAD_DIM], jk_out),
            (kv_ref.at[:, HEAD_DIM:], jv_out),
            (drift_ref, drift_out),
        ))
    ]
    half = HEAD_DIM // 2
    lane = lax.rem(iota((1, HEAD_DIM), 1), half)
    freq = jnp.zeros((1, HEAD_DIM), jnp.float32)
    for i, value in enumerate(inverse_freq()):
        freq = jnp.where(lane == i, value, freq)
    for copy in copies[:3]:
        copy.wait()
    groups = offsets_ref.shape[1]
    own_start = jnp.sum(
        jnp.where(
            iota((1, groups), 1) == lax.axis_index("ctx"), offsets_ref[...].astype(jnp.float32), 0.0
        ),
        axis=1,
        keepdims=True,
    )
    count = count_ref[...]
    index_row = index_ref[...]
    index_col = column_of(index_row.astype(jnp.float32))
    slot_angle = (index_col + own_start) * freq
    group_angle = own_start * freq
    sign = jnp.where(iota((1, HEAD_DIM), 1) < half, -1.0, 1.0)
    slot_cos, slot_sin = jnp.cos(slot_angle), jnp.sin(slot_angle) * sign
    group_cos, group_sin = jnp.cos(group_angle), jnp.sin(group_angle) * sign

    def turn(rows, cosine, sine):
        x = rows.astype(jnp.float32)
        return (x * cosine + pltpu.roll(x, half, 1) * sine).astype(jnp.bfloat16)

    copies[3].wait()
    for h in range(HEADS_PER):
        head = turn(q_ref[:, h * HEAD_DIM : (h + 1) * HEAD_DIM], slot_cos, slot_sin)
        for y in range(Y):
            copies_ref[y, h * SLOTS : (h + 1) * SLOTS, :] = head
    sends[0].start()

    for copy in copies[4:]:
        copy.wait()
    turned = turn(ck_ref[...], group_cos, group_sin)
    fresh = turn(fk_ref[...], slot_cos, slot_sin)
    cached_values = cv_ref[...]
    fresh_values = fv_ref[...]

    live = iota((1, SLOTS), 1) < count
    chosen = jnp.where(live, index_row, -1)
    picker = jnp.where(iota((GROUP_LEN, SLOTS), 0) == chosen, 1.0, 0.0)
    covered = jnp.sum(picker, axis=1, keepdims=True) > 0.0
    picker = picker.astype(jnp.bfloat16)
    joined_keys = jnp.where(
        covered,
        jnp.dot(picker, fresh, preferred_element_type=jnp.float32),
        turned.astype(jnp.float32),
    ).astype(jnp.bfloat16)
    joined_values = jnp.where(
        covered,
        jnp.dot(picker, fresh_values, preferred_element_type=jnp.float32),
        cached_values.astype(jnp.float32),
    ).astype(jnp.bfloat16)
    kv_ref[:, :HEAD_DIM] = joined_keys
    kv_ref[:, HEAD_DIM:] = joined_values
    for send in sends[1:4]:
        send.start()

    reader = jnp.where(
        iota((SLOTS, GROUP_LEN), 1).astype(jnp.float32) == index_col, 1.0, 0.0
    ).astype(jnp.bfloat16)
    key_gap = fresh.astype(jnp.float32) - jnp.dot(
        reader, turned, preferred_element_type=jnp.float32
    )
    value_gap = fresh_values.astype(jnp.float32) - jnp.dot(
        reader, cached_values, preferred_element_type=jnp.float32
    )
    squares = jnp.sum(key_gap * key_gap + value_gap * value_gap, axis=1, keepdims=True)
    drift_row = row_of(jnp.broadcast_to(squares, (SLOTS, SLOTS)))
    drift_ref[...] = drift_row
    sends[4].start()
    for send in sends:
        send.wait()


def attend_kernel(
    index_ref, q_ref, own_ref, other_ref, out_hbm, values, own_limit, other_limit,
    scores_even, scores_odd, peaks_even, peaks_odd, out_ref, left,
):
    me = lax.axis_index("ctx")
    core = lax.rem(me, CORES)
    y_own = lax.rem(me // CORES, Y)
    z_own = me // (CORES * Y)
    gathered = Z_HI * GROUP_LEN
    sources = (own_ref, own_limit), (other_ref, other_limit)

    index_col = column_of(index_ref[...].astype(jnp.float32))
    slot = lax.rem(iota((SLOTS, ROWS), 1), SLOTS)
    own_index = jnp.sum(
        jnp.where(slot == iota((SLOTS, ROWS), 0), index_col, 0.0), axis=0, keepdims=True
    )
    before = z_own * GROUP_LEN - 1
    full = before + GROUP_LEN
    for place in range(Y):
        y = jnp.where(core == 1, QUERY_ORDERS[1][place], QUERY_ORDERS[0][place])
        lanes = slice(place * ROWS, (place + 1) * ROWS)
        beside = jnp.where(y_own < y, full, before)
        own_limit[:, lanes] = jnp.where(
            y == y_own, own_index.astype(jnp.int32) + (before + 1), beside
        )
        other_limit[:, lanes] = jnp.full(
            (1, ROWS), jnp.where(jnp.logical_and(y == y_own, core == 1), full, beside), jnp.int32
        )

    def score(step, size, masked, scores, peaks):
        lanes = pl.ds(pl.multiple_of(step * STEP, STEP), STEP)
        queries = q_ref[lanes, :]
        top = None
        for part, (source, limit_ref) in enumerate(sources):
            limit = limit_ref[:, lanes]
            for at in range(0, size, CHUNK):
                found = lax.dot_general(
                    source[at : at + CHUNK, :HEAD_DIM],
                    queries,
                    (((1,), (1,)), ((), ())),
                    preferred_element_type=jnp.float32,
                )
                if at + CHUNK > masked:
                    found = jnp.where(iota((CHUNK, STEP), 0) <= limit - at, found, NEG_FILL)
                scores[part * size + at : part * size + at + CHUNK, :] = found
                for row in range(0, CHUNK, WIDE):
                    tile = found[row : row + WIDE]
                    top = tile if top is None else jnp.maximum(top, tile)
        peaks[...] = jnp.max(top, axis=0, keepdims=True)

    def weigh(step, size, scores, peaks):
        peak = peaks[...]
        total = jnp.zeros((HEAD_DIM + ONES, STEP), jnp.float32)
        for part in range(2):
            weights = []
            for at in range(part * size, (part + 1) * size, CHUNK):
                weight = jnp.exp2((scores[at : at + CHUNK, :] - peak) * EXP2_SCALE)
                weights.append(weight.astype(jnp.bfloat16))
            total = total + jnp.dot(
                values[:, part * gathered : part * gathered + size],
                jnp.concatenate(weights, axis=0),
                preferred_element_type=jnp.float32,
            )
        mass = total[HEAD_DIM : HEAD_DIM + 1]
        outcome = (total[:HEAD_DIM] * (1.0 / mass)).astype(jnp.bfloat16)
        rest = jnp.where(peak > 0.5 * NEG_FILL, peak * SCORE_SCALE + jnp.log(mass), NEG_FILL)
        stat = jnp.zeros((STAT_ROWS, STEP), jnp.float32)
        row = iota((STAT_ROWS, STEP), 0)
        for piece in range(3):
            part = rest.astype(jnp.bfloat16).astype(jnp.float32)
            stat = jnp.where(row == piece, part, stat)
            rest = rest - part
        stat = stat.astype(jnp.bfloat16)
        for half in range(STEP // HEAD_DIM):
            tile = step * (STEP // HEAD_DIM) + half
            place = tile // (ROWS // HEAD_DIM)
            lanes = pl.ds(
                pl.multiple_of(lax.rem(tile, ROWS // HEAD_DIM) * HEAD_DIM, HEAD_DIM), HEAD_DIM
            )
            columns = slice(half * HEAD_DIM, (half + 1) * HEAD_DIM)
            out_ref[place, :HEAD_DIM, lanes] = outcome[:, columns]
            out_ref[place, HEAD_DIM:, lanes] = stat[:, columns]

    def all_steps(size, masked):
        even, odd = (scores_even, peaks_even), (scores_odd, peaks_odd)
        steps = Y * ROWS // STEP
        score(0, size, masked, *even)
        for part, (source, _) in enumerate(sources):
            values[:HEAD_DIM, part * gathered : part * gathered + size] = source[:size, HEAD_DIM:].T
        values[HEAD_DIM:, :] = jnp.ones((ONES, CORES * gathered), jnp.bfloat16)

        def two(pair, carry):
            step = 2 * pair
            score(step + 1, size, masked, *odd)
            weigh(step, size, *even)
            score(step + 2, size, masked, *even)
            weigh(step + 1, size, *odd)
            return carry

        lax.fori_loop(0, steps // 2 - 1, two, 0)
        done = (steps - 2) * STEP // ROWS
        first = pltpu.make_async_copy(out_ref.at[:done], out_hbm.at[:done], left.at[0])
        first.start()
        score(steps - 1, size, masked, *odd)
        weigh(steps - 2, size, *even)
        weigh(steps - 1, size, *odd)
        last = pltpu.make_async_copy(out_ref.at[done:], out_hbm.at[done:], left.at[1])
        last.start()
        first.wait()
        last.wait()

    @pl.when(z_own == Z_HI - 1)
    def _():
        all_steps(gathered, gathered - GROUP_LEN)

    @pl.when(z_own != Z_HI - 1)
    def _():
        all_steps(SHORT, 0)


def merge_kernel(count_ref, parts_ref, out_ref):
    live = iota((SLOTS, HEAD_DIM), 0) < count_ref[...]
    levels = []
    for y in range(Y):
        stat = parts_ref[y, HEAD_DIM:, :].astype(jnp.float32)
        levels.append(stat[0:1] + stat[1:2] + stat[2:3])
    top = functools.reduce(jnp.maximum, levels)
    shares = [jnp.exp(level - top) for level in levels]
    scale = 1.0 / functools.reduce(jnp.add, shares)
    for k in range(ROWS // HEAD_DIM):
        lanes = slice(k * HEAD_DIM, (k + 1) * HEAD_DIM)
        total = jnp.zeros((HEAD_DIM, HEAD_DIM), jnp.float32)
        for y in range(Y):
            part = parts_ref[y, :HEAD_DIM, lanes].astype(jnp.float32)
            total = total + (shares[y] * scale)[:, lanes] * part
        rows = total.T
        for at in range(0, HEAD_DIM, 16):
            head, slot = divmod(k * HEAD_DIM + at, SLOTS)
            found = jnp.where(live[slot : slot + 16], rows[at : at + 16], 0.0)
            out_ref[slot : slot + 16, head * HEAD_DIM : (head + 1) * HEAD_DIM] = found.astype(
                jnp.bfloat16
            )


def kernel_params(mib):
    return pltpu.CompilerParams(vmem_limit_bytes=mib << 20)


def shards(
    queries,
    cached_keys,
    cached_values,
    fresh_keys,
    fresh_values,
    recompute_index,
    recompute_count,
    group_offsets,
):
    bf16, f32 = jnp.bfloat16, jnp.float32
    shape = jax.ShapeDtypeStruct
    count = recompute_count.reshape(1, 1)
    copies, own_kv, joined_keys, joined_values, squares = pl.pallas_call(
        prepare_kernel,
        out_shape=(
            shape((Y, ROWS, HEAD_DIM), bf16),
            shape((GROUP_LEN, 2 * HEAD_DIM), bf16),
            shape((GROUP_LEN, HEAD_DIM), bf16),
            shape((GROUP_LEN, HEAD_DIM), bf16),
            shape((1, SLOTS), f32),
        ),
        in_specs=[HBM] * 8,
        out_specs=[HBM] * 5,
        scratch_shapes=[
            pltpu.VMEM((1, group_offsets.shape[0]), jnp.int32),
            pltpu.VMEM((1, 1), jnp.int32),
            pltpu.VMEM((1, SLOTS), jnp.int32),
            pltpu.VMEM((SLOTS, HEADS_PER * HEAD_DIM), bf16),
            pltpu.VMEM((GROUP_LEN, HEAD_DIM), bf16),
            pltpu.VMEM((GROUP_LEN, HEAD_DIM), bf16),
            pltpu.VMEM((SLOTS, HEAD_DIM), bf16),
            pltpu.VMEM((SLOTS, HEAD_DIM), bf16),
            pltpu.VMEM((Y, ROWS, HEAD_DIM), bf16),
            pltpu.VMEM((GROUP_LEN, 2 * HEAD_DIM), bf16),
            pltpu.VMEM((1, SLOTS), f32),
            pltpu.SemaphoreType.DMA((8,)),
            pltpu.SemaphoreType.DMA((5,)),
        ],
        name="prepare",
    )(
        group_offsets.reshape(1, -1), count, recompute_index,
        queries, cached_keys, cached_values, fresh_keys, fresh_values,
    )

    all_queries = lax.all_to_all(
        copies, "ctx", 0, 0, axis_index_groups=QUERY_GROUPS, tiled=True
    )
    core_kv = lax.all_gather(own_kv, "ctx", axis=0, axis_index_groups=KEY_GROUPS, tiled=True)
    other_kv = lax.ppermute(core_kv, "ctx", CORE_SWAP)

    score_shape = pltpu.VMEM((CORES * Z_HI * GROUP_LEN, STEP), f32)
    partial = pl.pallas_call(
        attend_kernel,
        out_shape=shape((Y, HEAD_DIM + STAT_ROWS, ROWS), bf16),
        in_specs=[VMEM] * 4,
        out_specs=HBM,
        scratch_shapes=[
            pltpu.VMEM((HEAD_DIM + ONES, CORES * Z_HI * GROUP_LEN), bf16),
            pltpu.VMEM((1, Y * ROWS), jnp.int32),
            pltpu.VMEM((1, Y * ROWS), jnp.int32),
            score_shape,
            score_shape,
            pltpu.VMEM((1, STEP), f32),
            pltpu.VMEM((1, STEP), f32),
            pltpu.VMEM((Y, HEAD_DIM + STAT_ROWS, ROWS), bf16),
            pltpu.SemaphoreType.DMA((2,)),
        ],
        compiler_params=kernel_params(28),
        name="attend",
    )(recompute_index, all_queries.reshape(Y * ROWS, HEAD_DIM), core_kv, other_kv)

    parts = lax.all_to_all(
        partial, "ctx", 0, 0, axis_index_groups=QUERY_GROUPS, tiled=True
    )
    squares = lax.all_gather(squares, "head", axis=0, tiled=True)
    drift = squares.sum(axis=0, keepdims=True)
    drift = drift / (2.0 * KV_HEADS * HEAD_DIM)
    drift = jnp.where(iota((1, SLOTS), 1) < recompute_count[0], drift, 0.0)

    attention = pl.pallas_call(
        merge_kernel,
        out_shape=shape((SLOTS, HEADS_PER * HEAD_DIM), bf16),
        in_specs=[VMEM, VMEM],
        out_specs=VMEM,
        compiler_params=kernel_params(16),
        name="merge",
    )(count, parts)
    return (attention, joined_keys, joined_values, drift)


def solution(mesh):
    return jax.shard_map(
        shards,
        mesh=mesh,
        in_specs=(
            P("ctx", "head"),
            P("ctx", "head"),
            P("ctx", "head"),
            P("ctx", "head"),
            P("ctx", "head"),
            P("ctx", None),
            P("ctx"),
            P(),
        ),
        out_specs=(P("ctx", "head"), P("ctx", "head"), P("ctx", "head"), P("ctx", None)),
        check_vma=False,
    )
```

```python
import functools
import math

import jax
import jax.numpy as jnp
import numpy as np
from jax import lax
from jax.experimental import pallas as pl
from jax.experimental.pallas import tpu as pltpu
from jax.sharding import PartitionSpec as P


HEADS = 64
KV_HEADS = 8
HEAD_DIM = 128
HEADS_PER = HEADS // KV_HEADS
Z_HI, Y, CORES = 4, 8, 2
SLOTS = 48
GROUP_LEN = 320
ROWS = SLOTS * HEADS_PER
STAT_ROWS = 8
ONES = 16
STEP = 256
CHUNK = 256
WIDE = 64
SHORT = 1024
NEG_FILL = -1e30
EXP2_SCALE = math.log2(math.e) / math.sqrt(HEAD_DIM)
SCORE_SCALE = 1.0 / math.sqrt(HEAD_DIM)

VMEM = pl.BlockSpec(memory_space=pltpu.VMEM)
HBM = pl.BlockSpec(memory_space=pltpu.HBM)


def ctx_index(z_hi, y, core):
    return (z_hi * Y + y) * CORES + core


QUERY_ORDERS = [[7, 0, 6, 1, 5, 2, 4, 3]] * CORES
QUERY_GROUPS = [
    [ctx_index(z, y, c) for y in QUERY_ORDERS[c]] for z in range(Z_HI) for c in range(CORES)
]
KEY_GROUPS = [[ctx_index(z, y, c) for z in range(Z_HI)] for y in range(Y) for c in range(CORES)]
CORE_SWAP = [(i, i ^ 1) for i in range(Z_HI * Y * CORES)]


def inverse_freq():
    base = 1.0 / 500000.0 ** (np.arange(HEAD_DIM // 2) * 2.0 / HEAD_DIM)
    wavelength = 2.0 * np.pi / base
    smooth = (8192.0 / wavelength - 1.0) / 3.0
    blended = (1.0 - smooth) * base / 8.0 + smooth * base
    freq = np.where(wavelength < 2048.0, base, np.where(wavelength > 8192.0, base / 8.0, blended))
    return [float(value) for value in freq.astype(np.float32)]


def iota(shape, dim):
    return lax.broadcasted_iota(jnp.int32, shape, dim)


def column_of(row):
    n = row.shape[1]
    eye = iota((n, n), 0) == iota((n, n), 1)
    return jnp.sum(jnp.where(eye, jnp.broadcast_to(row, (n, n)), 0.0), axis=1, keepdims=True)


def row_of(wide):
    n = wide.shape[0]
    eye = iota((n, n), 0) == iota((n, n), 1)
    return jnp.sum(jnp.where(eye, wide, 0.0), axis=0, keepdims=True)


def prepare_kernel(
    offsets_hbm, count_hbm, index_hbm, q_hbm, ck_hbm, cv_hbm, fk_hbm, fv_hbm,
    q_out, kv_out, jk_out, jv_out, drift_out,
    offsets_ref, count_ref, index_ref, q_ref, ck_ref, cv_ref, fk_ref, fv_ref, copies_ref, kv_ref, drift_ref,
    arrived, left,
):
    copies = [
        pltpu.make_async_copy(source, target, arrived.at[i])
        for i, (source, target) in enumerate((
            (offsets_hbm, offsets_ref), (count_hbm, count_ref), (index_hbm, index_ref),
            (q_hbm, q_ref), (fk_hbm, fk_ref), (ck_hbm, ck_ref), (fv_hbm, fv_ref), (cv_hbm, cv_ref),
        ))
    ]
    for copy in copies:
        copy.start()
    sends = [
        pltpu.make_async_copy(source, target, left.at[i])
        for i, (source, target) in enumerate((
            (copies_ref, q_out),
            (kv_ref, kv_out),
            (kv_ref.at[:, :HEAD_DIM], jk_out),
            (kv_ref.at[:, HEAD_DIM:], jv_out),
            (drift_ref, drift_out),
        ))
    ]
    half = HEAD_DIM // 2
    lane = lax.rem(iota((1, HEAD_DIM), 1), half)
    freq = jnp.zeros((1, HEAD_DIM), jnp.float32)
    for i, value in enumerate(inverse_freq()):
        freq = jnp.where(lane == i, value, freq)
    for copy in copies[:3]:
        copy.wait()
    groups = offsets_ref.shape[1]
    own_start = jnp.sum(
        jnp.where(
            iota((1, groups), 1) == lax.axis_index("ctx"), offsets_ref[...].astype(jnp.float32), 0.0
        ),
        axis=1,
        keepdims=True,
    )
    count = count_ref[...]
    index_row = index_ref[...]
    index_col = column_of(index_row.astype(jnp.float32))
    slot_angle = (index_col + own_start) * freq
    group_angle = own_start * freq
    sign = jnp.where(iota((1, HEAD_DIM), 1) < half, -1.0, 1.0)
    slot_cos, slot_sin = jnp.cos(slot_angle), jnp.sin(slot_angle) * sign
    group_cos, group_sin = jnp.cos(group_angle), jnp.sin(group_angle) * sign

    def turn(rows, cosine, sine):
        x = rows.astype(jnp.float32)
        return (x * cosine + pltpu.roll(x, half, 1) * sine).astype(jnp.bfloat16)

    copies[3].wait()
    for h in range(HEADS_PER):
        head = turn(q_ref[:, h * HEAD_DIM : (h + 1) * HEAD_DIM], slot_cos, slot_sin)
        for y in range(Y):
            copies_ref[y, h * SLOTS : (h + 1) * SLOTS, :] = head
    sends[0].start()

    for copy in copies[4:]:
        copy.wait()
    turned = turn(ck_ref[...], group_cos, group_sin)
    fresh = turn(fk_ref[...], slot_cos, slot_sin)
    cached_values = cv_ref[...]
    fresh_values = fv_ref[...]

    live = iota((1, SLOTS), 1) < count
    chosen = jnp.where(live, index_row, -1)
    picker = jnp.where(iota((GROUP_LEN, SLOTS), 0) == chosen, 1.0, 0.0)
    covered = jnp.sum(picker, axis=1, keepdims=True) > 0.0
    picker = picker.astype(jnp.bfloat16)
    joined_keys = jnp.where(
        covered,
        jnp.dot(picker, fresh, preferred_element_type=jnp.float32),
        turned.astype(jnp.float32),
    ).astype(jnp.bfloat16)
    joined_values = jnp.where(
        covered,
        jnp.dot(picker, fresh_values, preferred_element_type=jnp.float32),
        cached_values.astype(jnp.float32),
    ).astype(jnp.bfloat16)
    kv_ref[:, :HEAD_DIM] = joined_keys
    kv_ref[:, HEAD_DIM:] = joined_values
    for send in sends[1:4]:
        send.start()

    reader = jnp.where(
        iota((SLOTS, GROUP_LEN), 1).astype(jnp.float32) == index_col, 1.0, 0.0
    ).astype(jnp.bfloat16)
    key_gap = fresh.astype(jnp.float32) - jnp.dot(
        reader, turned, preferred_element_type=jnp.float32
    )
    value_gap = fresh_values.astype(jnp.float32) - jnp.dot(
        reader, cached_values, preferred_element_type=jnp.float32
    )
    squares = jnp.sum(key_gap * key_gap + value_gap * value_gap, axis=1, keepdims=True)
    drift_row = row_of(jnp.broadcast_to(squares, (SLOTS, SLOTS)))
    drift_ref[...] = drift_row
    sends[4].start()
    for send in sends:
        send.wait()


def attend_kernel(
    index_ref, q_ref, own_ref, other_ref, out_hbm, values, own_limit, other_limit,
    scores_even, scores_odd, peaks_even, peaks_odd, out_ref, left,
):
    me = lax.axis_index("ctx")
    core = lax.rem(me, CORES)
    y_own = lax.rem(me // CORES, Y)
    z_own = me // (CORES * Y)
    gathered = Z_HI * GROUP_LEN
    sources = (own_ref, own_limit), (other_ref, other_limit)

    index_col = column_of(index_ref[...].astype(jnp.float32))
    slot = lax.rem(iota((SLOTS, ROWS), 1), SLOTS)
    own_index = jnp.sum(
        jnp.where(slot == iota((SLOTS, ROWS), 0), index_col, 0.0), axis=0, keepdims=True
    )
    before = z_own * GROUP_LEN - 1
    full = before + GROUP_LEN
    for place in range(Y):
        y = jnp.where(core == 1, QUERY_ORDERS[1][place], QUERY_ORDERS[0][place])
        lanes = slice(place * ROWS, (place + 1) * ROWS)
        beside = jnp.where(y_own < y, full, before)
        own_limit[:, lanes] = jnp.where(
            y == y_own, own_index.astype(jnp.int32) + (before + 1), beside
        )
        other_limit[:, lanes] = jnp.full(
            (1, ROWS), jnp.where(jnp.logical_and(y == y_own, core == 1), full, beside), jnp.int32
        )

    def score(step, size, masked, scores, peaks):
        lanes = pl.ds(pl.multiple_of(step * STEP, STEP), STEP)
        queries = q_ref[lanes, :]
        top = None
        for part, (source, limit_ref) in enumerate(sources):
            limit = limit_ref[:, lanes]
            for at in range(0, size, CHUNK):
                found = lax.dot_general(
                    source[at : at + CHUNK, :HEAD_DIM],
                    queries,
                    (((1,), (1,)), ((), ())),
                    preferred_element_type=jnp.float32,
                )
                if at + CHUNK > masked:
                    found = jnp.where(iota((CHUNK, STEP), 0) <= limit - at, found, NEG_FILL)
                scores[part * size + at : part * size + at + CHUNK, :] = found
                for row in range(0, CHUNK, WIDE):
                    tile = found[row : row + WIDE]
                    top = tile if top is None else jnp.maximum(top, tile)
        peaks[...] = jnp.max(top, axis=0, keepdims=True)

    def weigh(step, size, scores, peaks):
        peak = peaks[...]
        total = jnp.zeros((HEAD_DIM + ONES, STEP), jnp.float32)
        for part in range(2):
            weights = []
            for at in range(part * size, (part + 1) * size, CHUNK):
                weight = jnp.exp2((scores[at : at + CHUNK, :] - peak) * EXP2_SCALE)
                weights.append(weight.astype(jnp.bfloat16))
            total = total + jnp.dot(
                values[:, part * gathered : part * gathered + size],
                jnp.concatenate(weights, axis=0),
                preferred_element_type=jnp.float32,
            )
        mass = total[HEAD_DIM : HEAD_DIM + 1]
        outcome = (total[:HEAD_DIM] * (1.0 / mass)).astype(jnp.bfloat16)
        rest = jnp.where(peak > 0.5 * NEG_FILL, peak * SCORE_SCALE + jnp.log(mass), NEG_FILL)
        stat = jnp.zeros((STAT_ROWS, STEP), jnp.float32)
        row = iota((STAT_ROWS, STEP), 0)
        for piece in range(3):
            part = rest.astype(jnp.bfloat16).astype(jnp.float32)
            stat = jnp.where(row == piece, part, stat)
            rest = rest - part
        stat = stat.astype(jnp.bfloat16)
        for half in range(STEP // HEAD_DIM):
            tile = step * (STEP // HEAD_DIM) + half
            place = tile // (ROWS // HEAD_DIM)
            lanes = pl.ds(
                pl.multiple_of(lax.rem(tile, ROWS // HEAD_DIM) * HEAD_DIM, HEAD_DIM), HEAD_DIM
            )
            columns = slice(half * HEAD_DIM, (half + 1) * HEAD_DIM)
            out_ref[place, :HEAD_DIM, lanes] = outcome[:, columns]
            out_ref[place, HEAD_DIM:, lanes] = stat[:, columns]

    def all_steps(size, masked):
        even, odd = (scores_even, peaks_even), (scores_odd, peaks_odd)
        steps = Y * ROWS // STEP
        score(0, size, masked, *even)
        for part, (source, _) in enumerate(sources):
            values[:HEAD_DIM, part * gathered : part * gathered + size] = source[:size, HEAD_DIM:].T
        values[HEAD_DIM:, :] = jnp.ones((ONES, CORES * gathered), jnp.bfloat16)

        def two(pair, carry):
            step = 2 * pair
            score(step + 1, size, masked, *odd)
            weigh(step, size, *even)
            score(step + 2, size, masked, *even)
            weigh(step + 1, size, *odd)
            return carry

        lax.fori_loop(0, steps // 2 - 1, two, 0)
        done = (steps - 2) * STEP // ROWS
        first = pltpu.make_async_copy(out_ref.at[:done], out_hbm.at[:done], left.at[0])
        first.start()
        score(steps - 1, size, masked, *odd)
        weigh(steps - 2, size, *even)
        weigh(steps - 1, size, *odd)
        last = pltpu.make_async_copy(out_ref.at[done:], out_hbm.at[done:], left.at[1])
        last.start()
        first.wait()
        last.wait()

    @pl.when(z_own == Z_HI - 1)
    def _():
        all_steps(gathered, gathered - GROUP_LEN)

    @pl.when(z_own != Z_HI - 1)
    def _():
        all_steps(SHORT, 0)


def merge_kernel(count_ref, parts_ref, out_ref):
    live = iota((SLOTS, HEAD_DIM), 0) < count_ref[...]
    levels = []
    for y in range(Y):
        stat = parts_ref[y, HEAD_DIM:, :].astype(jnp.float32)
        levels.append(stat[0:1] + stat[1:2] + stat[2:3])
    top = functools.reduce(jnp.maximum, levels)
    shares = [jnp.exp(level - top) for level in levels]
    scale = 1.0 / functools.reduce(jnp.add, shares)
    for k in range(ROWS // HEAD_DIM):
        lanes = slice(k * HEAD_DIM, (k + 1) * HEAD_DIM)
        total = jnp.zeros((HEAD_DIM, HEAD_DIM), jnp.float32)
        for y in range(Y):
            part = parts_ref[y, :HEAD_DIM, lanes].astype(jnp.float32)
            total = total + (shares[y] * scale)[:, lanes] * part
        rows = total.T
        for at in range(0, HEAD_DIM, 16):
            head, slot = divmod(k * HEAD_DIM + at, SLOTS)
            found = jnp.where(live[slot : slot + 16], rows[at : at + 16], 0.0)
            out_ref[slot : slot + 16, head * HEAD_DIM : (head + 1) * HEAD_DIM] = found.astype(
                jnp.bfloat16
            )


def kernel_params(mib):
    return pltpu.CompilerParams(vmem_limit_bytes=mib << 20)


def shards(
    queries,
    cached_keys,
    cached_values,
    fresh_keys,
    fresh_values,
    recompute_index,
    recompute_count,
    group_offsets,
):
    bf16, f32 = jnp.bfloat16, jnp.float32
    shape = jax.ShapeDtypeStruct
    count = recompute_count.reshape(1, 1)
    copies, own_kv, joined_keys, joined_values, squares = pl.pallas_call(
        prepare_kernel,
        out_shape=(
            shape((Y, ROWS, HEAD_DIM), bf16),
            shape((GROUP_LEN, 2 * HEAD_DIM), bf16),
            shape((GROUP_LEN, HEAD_DIM), bf16),
            shape((GROUP_LEN, HEAD_DIM), bf16),
            shape((1, SLOTS), f32),
        ),
        in_specs=[HBM] * 8,
        out_specs=[HBM] * 5,
        scratch_shapes=[
            pltpu.VMEM((1, group_offsets.shape[0]), jnp.int32),
            pltpu.VMEM((1, 1), jnp.int32),
            pltpu.VMEM((1, SLOTS), jnp.int32),
            pltpu.VMEM((SLOTS, HEADS_PER * HEAD_DIM), bf16),
            pltpu.VMEM((GROUP_LEN, HEAD_DIM), bf16),
            pltpu.VMEM((GROUP_LEN, HEAD_DIM), bf16),
            pltpu.VMEM((SLOTS, HEAD_DIM), bf16),
            pltpu.VMEM((SLOTS, HEAD_DIM), bf16),
            pltpu.VMEM((Y, ROWS, HEAD_DIM), bf16),
            pltpu.VMEM((GROUP_LEN, 2 * HEAD_DIM), bf16),
            pltpu.VMEM((1, SLOTS), f32),
            pltpu.SemaphoreType.DMA((8,)),
            pltpu.SemaphoreType.DMA((5,)),
        ],
        name="prepare",
    )(
        group_offsets.reshape(1, -1), count, recompute_index,
        queries, cached_keys, cached_values, fresh_keys, fresh_values,
    )

    all_queries = lax.all_to_all(
        copies, "ctx", 0, 0, axis_index_groups=QUERY_GROUPS, tiled=True
    )
    core_kv = lax.all_gather(own_kv, "ctx", axis=0, axis_index_groups=KEY_GROUPS, tiled=True)
    other_kv = lax.ppermute(core_kv, "ctx", CORE_SWAP)

    score_shape = pltpu.VMEM((CORES * Z_HI * GROUP_LEN, STEP), f32)
    partial = pl.pallas_call(
        attend_kernel,
        out_shape=shape((Y, HEAD_DIM + STAT_ROWS, ROWS), bf16),
        in_specs=[VMEM] * 4,
        out_specs=HBM,
        scratch_shapes=[
            pltpu.VMEM((HEAD_DIM + ONES, CORES * Z_HI * GROUP_LEN), bf16),
            pltpu.VMEM((1, Y * ROWS), jnp.int32),
            pltpu.VMEM((1, Y * ROWS), jnp.int32),
            score_shape,
            score_shape,
            pltpu.VMEM((1, STEP), f32),
            pltpu.VMEM((1, STEP), f32),
            pltpu.VMEM((Y, HEAD_DIM + STAT_ROWS, ROWS), bf16),
            pltpu.SemaphoreType.DMA((2,)),
        ],
        compiler_params=kernel_params(28),
        name="attend",
    )(recompute_index, all_queries.reshape(Y * ROWS, HEAD_DIM), core_kv, other_kv)

    parts = lax.all_to_all(
        partial, "ctx", 0, 0, axis_index_groups=QUERY_GROUPS, tiled=True
    )
    for step in (1, 2):
        squares = squares + lax.ppermute(squares, "head", [(i, i ^ step) for i in range(KV_HEADS)])
    other = lax.ppermute(squares, "head", [(i, i ^ 4) for i in range(KV_HEADS)])
    drift = (squares + other) / (2.0 * KV_HEADS * HEAD_DIM)
    drift = jnp.where(iota((1, SLOTS), 1) < recompute_count[0], drift, 0.0)

    attention = pl.pallas_call(
        merge_kernel,
        out_shape=shape((SLOTS, HEADS_PER * HEAD_DIM), bf16),
        in_specs=[VMEM, VMEM],
        out_specs=VMEM,
        compiler_params=kernel_params(16),
        name="merge",
    )(count, parts)
    return (attention, joined_keys, joined_values, drift)


def solution(mesh):
    return jax.shard_map(
        shards,
        mesh=mesh,
        in_specs=(
            P("ctx", "head"),
            P("ctx", "head"),
            P("ctx", "head"),
            P("ctx", "head"),
            P("ctx", "head"),
            P("ctx", None),
            P("ctx"),
            P(),
        ),
        out_specs=(P("ctx", "head"), P("ctx", "head"), P("ctx", "head"), P("ctx", None)),
        check_vma=False,
    )
```
